512 devices in a mesh: dp: 64 (over y, x, z_lo), seq: 8 (over z_hi, core).
Axes of the slice: x: 4, y: 8, z: 8 (z_hi: 4, z_lo: 2; z = z_hi * 2 + z_lo), core: 2. Of those that a mesh axis runs over, the one named last changes fastest.
Arguments:
- query_rows: bfloat16 [73728, 2048], P(('dp', 'seq')), may hold values from -500 to 500
- key_rows: bfloat16 [73728, 2048], P(('dp', 'seq')), may hold values from -5 to 5
- value_rows: bfloat16 [73728, 2048], P(('dp', 'seq')), may hold values from -6 to 6
- windows: int32 [16, 3], replicated, may hold values from 1 to 3, as said below
- out_weight: bfloat16 [2048, 3072], P('dp', 'seq'), may hold values from -0.125 to 0.125
- gate_scale: bfloat16 [64, 3072], P('dp', 'seq'), may hold values from 0.5 to 1.5
- out_grad: bfloat16 [73728, 3072], P('dp', 'seq'), may hold values from -0.0234375 to 0.0234375
Outputs:
- block_out: bfloat16 [73728, 3072], P('dp', 'seq')
- weight_grad: float32 [2048, 3072], P('dp', 'seq')
The draws below stay inside these ranges and needn't reach their ends.
Inputs may be any that keep to these rules, and one draw needn't show every extreme that they name: `windows`: one head has extent 3 along all three dimensions.
All inputs are finite; a program needn't handle non-finite values.
Results may differ from the reference program's by a relative error of at most 0.0057.
Values may be sent and summed in bfloat16 or wider, within the bound.
A program may use at most 128 MiB of HBM per device.

```python
import math
import jax
import jax.numpy as jnp
from jax import lax

D = 3072
HEADS = 16
HEAD_DIM = 128
GH = 3
GW = 4
EXT = 3
GT = 2
HD = 2048
TILE = 48
NT = 24
CLIP_TOK = 1152
CLIPS = 64
TOKENS = 73728


def shared_keys(key):
    raw = jax.random.normal(jax.random.fold_in(key, 7), (TOKENS, HD), jnp.float32)
    return jnp.clip(raw, -5.0, 5.0)


def draw_key_rows(key, part):
    base = shared_keys(key)
    return base.astype(jnp.bfloat16)


def draw_query_rows(key, part):
    own = jnp.clip(jax.random.normal(jax.random.fold_in(key, 13), (TOKENS, HD), jnp.float32), -5.0, 5.0)
    return own.astype(jnp.bfloat16)


def draw_windows(key, part):
    extent_key, head_key = jax.random.split(jax.random.fold_in(key, 21))
    extent = jax.random.randint(extent_key, (HEADS, 3), 1, EXT + 1).astype(jnp.int32)
    widest = jax.random.randint(head_key, (), 0, HEADS).astype(jnp.int32)
    head_id = jnp.arange(HEADS).astype(jnp.int32)
    extent = jnp.where(head_id[:, None] == widest, EXT, extent)
    return extent.astype(jnp.int32)


def steps_of(stream_key, shape, cuts, smallest, largest):
    level = 1.0
    for axis_at, parts in cuts:
        heights = jax.random.uniform(jax.random.fold_in(jax.random.fold_in(stream_key, 6), axis_at), (parts,), jnp.float32, smallest / len(cuts), largest / len(cuts))
        level = level * jnp.repeat(jnp.exp(heights), shape[axis_at] // parts).reshape((-1,) + (1,) * (len(shape) - 1 - axis_at))
    return level


def normal_values(own_key, dims, scale, reach, shards=(), kind=jnp.bfloat16):
    array = jax.random.normal(own_key, dims, jnp.float32) * scale
    if len(shards) > 0:
        array = steps_of(own_key, dims, shards, -0.22, 0.18) * array
    return jnp.clip(array, min=-reach, max=reach).astype(kind)


def setup_inputs(seed: int = 0) -> dict:
    streams_of = jax.random.split(jax.random.key(seed), 8)
    return {
        "query_rows": draw_query_rows(jax.random.fold_in(streams_of[7], 71), 0),
        "key_rows": draw_key_rows(jax.random.fold_in(streams_of[7], 71), 0),
        "value_rows": normal_values(streams_of[2], (TOKENS, HD), 1.0, 6.0, ((0, 512),)),
        "windows": draw_windows(jax.random.fold_in(streams_of[7], 71), 0),
        "out_weight": normal_values(streams_of[4], (HD, D), HD ** -0.5, 0.125, ((0, 64), (1, 8))),
        "gate_scale": jnp.clip(0.5 + 1.0 * jax.random.uniform(streams_of[5], (CLIPS, D), jnp.float32) ** steps_of(streams_of[5], (CLIPS, D), ((0, 64), (1, 8)), -0.2, 0.2), 0.5, 1.5).astype(jnp.bfloat16),
        "out_grad": normal_values(streams_of[6], (TOKENS, D), TOKENS ** -0.5, 0.0234375, ((0, 64), (1, 8))),
    }


def grid_limits():
    return (GT, GH, GW)

def tile_coords(length):
    position = jnp.arange(length).astype(jnp.int32)
    tile_id = position // TILE
    plane_size = GH * GW
    return jnp.stack([tile_id // plane_size, tile_id // GW % GH, tile_id % GW])

def head_windows(windows):
    limits = grid_limits()
    tile_id = jnp.arange(NT).astype(jnp.int32)
    coords = jnp.stack([tile_id // (GH * GW), tile_id // GW % GH, tile_id % GW])
    starts = []
    extents = []
    for axis_no in range(3):
        extent = jnp.minimum(windows[:, axis_no], limits[axis_no]).astype(jnp.int32)[:, None]
        start = jnp.clip(coords[axis_no][None, :] - (extent - 1) // 2, 0, limits[axis_no] - extent)
        starts.append(start.astype(jnp.int32))
        extents.append(extent)
    return (jnp.stack(starts), jnp.stack(extents))

def clip_attention(query_part, key_part, value_part, starts, extents):
    count = query_part.shape[0]
    row_block = math.gcd(count, 512)
    blocks = count // row_block
    score_scale = 1.0 / math.sqrt(HEAD_DIM)
    key_coords = tile_coords(count)
    query_blocks = query_part.astype(jnp.float32).reshape(blocks, row_block, HEADS, HEAD_DIM)
    key_heads = key_part.astype(jnp.float32).reshape(count, HEADS, HEAD_DIM)
    value_heads = value_part.astype(jnp.float32).reshape(count, HEADS, HEAD_DIM)
    firsts = (jnp.arange(blocks) * row_block).astype(jnp.int32)

    def one_block(operands):
        query_block, first_row = operands
        query_tiles = (first_row + jnp.arange(row_block).astype(jnp.int32)) // TILE
        visible = jnp.ones((HEADS, row_block, count), dtype=bool)
        for axis_no in range(3):
            lower = jnp.take(starts[axis_no], query_tiles, axis=1)[:, :, None]
            upper = lower + extents[axis_no][:, :, None]
            column = key_coords[axis_no][None, None, :]
            visible = visible & (column >= lower) & (column < upper)
        scores = jnp.einsum('qhd,khd->hqk', query_block, key_heads) * score_scale
        scores = jnp.where(visible, scores, -jnp.inf)
        row_peak = lax.optimization_barrier(jnp.max(scores, axis=-1, keepdims=True))
        weights = jnp.exp(scores - row_peak)
        denominator = lax.optimization_barrier(jnp.sum(weights, axis=-1, keepdims=True))
        weights_low = (weights / denominator).astype(jnp.bfloat16)
        blended = jnp.einsum('hqk,khd->qhd', weights_low.astype(jnp.float32), value_heads)
        return blended.astype(jnp.bfloat16).reshape(row_block, HD)
    return lax.map(one_block, (query_blocks, firsts)).reshape(count, HD)

def reference(query_rows, key_rows, value_rows, windows, out_weight, gate_scale, out_grad):
    clip_count = gate_scale.shape[0]
    starts, extents = head_windows(windows)
    query_clips = query_rows.reshape(clip_count, CLIP_TOK, HD)
    key_clips = key_rows.reshape(clip_count, CLIP_TOK, HD)
    value_clips = value_rows.reshape(clip_count, CLIP_TOK, HD)
    grad_clips = out_grad.reshape(clip_count, CLIP_TOK, D)

    def per_clip(carried, operands):
        query_part, key_part, value_part, gate_row, grad_part = operands
        attention = clip_attention(query_part, key_part, value_part, starts, extents)
        projected = jnp.dot(attention, out_weight, preferred_element_type=jnp.float32)
        gate_wide = gate_row.astype(jnp.float32)
        result = (projected * gate_wide).astype(jnp.bfloat16)
        grad_proj = (grad_part.astype(jnp.float32) * gate_wide).astype(jnp.bfloat16)
        carried = carried + lax.dot_general(attention, grad_proj, (((0,), (0,)), ((), ())), preferred_element_type=jnp.float32)
        return (carried, result)
    initial = jnp.zeros((HD, D), jnp.float32)
    weight_grad, outputs = lax.scan(per_clip, initial, (query_clips, key_clips, value_clips, gate_scale, grad_clips))
    return (outputs.reshape(TOKENS, D), weight_grad)
```

```python
import math

import jax
import jax.numpy as jnp
from jax import lax
from jax.experimental import pallas as pl
from jax.experimental.pallas import tpu as pltpu
from jax.sharding import PartitionSpec as P

HEAD_DIM = 128
GT, GH, GW = 2, 3, 4
TILE = 48
NT = 24
TOK = 1152
ROWS = 144
NY, NX, NZ = 8, 4, 2
NZH = 4
NS = 8
COLS = 384
WROWS = 32
HALF = TOK // 2
HIDE = -(2.0**100)
MESH = pl.DeviceIdType.MESH
SCALE2 = math.log2(math.e) / math.sqrt(HEAD_DIM)


def kernel(
    q_ref, k_ref, v_ref, win_ref, w_ref, gate_ref, og_ref,
    out_ref, wg_ref,
    qkv, onehot, bias, att, wbuf, og, gpt, acc, gf, xs, xr, ys, yr, yo, zs, zr,
    qs_sem, qr_sem, loc_sem, wz_sem, wy_s, wy_r, wx_s, wx_r,
    agd_s, agd_r, agf_s, agf_r, agc_s, agc_r, xs_sem, xr_sem, ys_sem, yr_sem, zs_sem,
):
    dp = lax.axis_index("dp")
    sq = lax.axis_index("seq")
    zl = lax.rem(dp, NZ)
    x = lax.rem(dp // NZ, NX)
    y = dp // (NZ * NX)
    zh = sq // 2
    c = lax.rem(sq, 2)

    def dpi(yy, xx, zz):
        return (yy * NX + xx) * NZ + zz

    def sqi(zz, cc):
        return lax.rem(zz + 2 * NZH, NZH) * 2 + cc

    bar = pltpu.get_barrier_semaphore()

    def greet(device):
        pl.semaphore_signal(bar, 1, device_id=device, device_id_type=MESH)

    for r in range(1, NS):
        greet((dp, lax.rem(sq + r, NS)))
    for r in range(1, NX):
        greet((dpi(y, lax.rem(x + r, NX), zl), sq))
    for r in range(1, NY):
        greet((dpi(lax.rem(y + r, NY), x, zl), sq))
    greet((dpi(y, x, 1 - zl), sq))
    pl.semaphore_wait(bar, (NS - 1) + (NX - 1) + (NY - 1) + 1)

    w_local = pltpu.make_async_copy(w_ref, wbuf.at[y, x, zl], loc_sem.at[0])
    w_local.start()
    w_z = pltpu.make_async_remote_copy(
        w_ref, wbuf.at[y, x, zl], wz_sem.at[0], wz_sem.at[1],
        device_id=(dpi(y, x, 1 - zl), sq), device_id_type=MESH)
    w_z.start()
    og_copy = pltpu.make_async_copy(og_ref, og, loc_sem.at[1])
    og_copy.start()

    tensors = (q_ref, k_ref, v_ref)

    def qkv_copy(h, t, r):
        dest = lax.rem(sq + r, NS)
        src = tensors[t].at[:, pl.ds(pl.multiple_of(dest * 256 + h * 128, 128), 128)]
        return pltpu.make_async_remote_copy(
            src, qkv.at[h, t, pl.ds(pl.multiple_of(sq * ROWS, 16), ROWS)],
            qs_sem.at[h, t, r], qr_sem.at[h, t, r],
            device_id=(dp, dest), device_id_type=MESH)

    def qkv_own(h, t):
        src = tensors[t].at[:, pl.ds(pl.multiple_of(sq * 256 + h * 128, 128), 128)]
        return pltpu.make_async_copy(
            src, qkv.at[h, t, pl.ds(pl.multiple_of(sq * ROWS, 16), ROWS)], qr_sem.at[h, t, 0])

    def qkv_wait(h, t, r):
        source = lax.rem(sq + NS - r, NS)
        land = qkv.at[h, t, pl.ds(pl.multiple_of(source * ROWS, 16), ROWS)]
        pltpu.make_async_remote_copy(
            land, land, qs_sem.at[h, t, r], qr_sem.at[h, t, r],
            device_id=(dp, source), device_id_type=MESH).wait_recv()

    for h in range(2):
        def start_one(r, carry, h=h):
            for t in range(3):
                qkv_copy(h, t, r).start()
            return carry
        lax.fori_loop(1, NS, start_one, 0)
        for t in range(3):
            qkv_own(h, t).start()

    lane = lax.broadcasted_iota(jnp.int32, (TOK, 128), 1)
    tile = lax.broadcasted_iota(jnp.int32, (TOK, 128), 0) // TILE
    onehot[...] = jnp.where(lane == tile, 1.0, 0.0).astype(jnp.bfloat16)
    limits = (GT, GH, GW)
    q_at = (tile // (GH * GW), tile // GW % GH, tile % GW)
    k_at = (lane // (GH * GW), lane // GW % GH, lane % GW)
    for h in range(2):
        inside = lane < NT
        for d in range(3):
            extent = jnp.minimum(win_ref[2 * sq + h, d], limits[d])
            first = jnp.clip(q_at[d] - (extent - 1) // 2, 0, limits[d] - extent)
            inside = inside & (k_at[d] >= first) & (k_at[d] < first + extent)
        bias[h] = jnp.where(inside | (lane >= NT), 0.0, HIDE).astype(jnp.bfloat16)

    w_local.wait()
    w_z.wait_recv()

    def wy_copy(r):
        dest = lax.rem(y + r, NY)
        return pltpu.make_async_remote_copy(
            wbuf.at[y, x], wbuf.at[y, x], wy_s.at[r], wy_r.at[r],
            device_id=(dpi(dest, x, zl), sq), device_id_type=MESH)

    def wy_wait(r):
        land = wbuf.at[lax.rem(y + NY - r, NY), x]
        pltpu.make_async_remote_copy(
            land, land, wy_s.at[r], wy_r.at[r],
            device_id=(dpi(y, x, zl), sq), device_id_type=MESH).wait_recv()

    def wx_copy(r):
        dest = lax.rem(x + r, NX)
        return pltpu.make_async_remote_copy(
            wbuf.at[:, x], wbuf.at[:, x], wx_s.at[r], wx_r.at[r],
            device_id=(dpi(y, dest, zl), sq), device_id_type=MESH)

    def wx_wait(r):
        land = wbuf.at[:, lax.rem(x + NX - r, NX)]
        pltpu.make_async_remote_copy(
            land, land, wx_s.at[r], wx_r.at[r],
            device_id=(dpi(y, x, zl), sq), device_id_type=MESH).wait_recv()

    for r in range(1, NY):
        wy_copy(r).start()

    og_copy.wait()
    gate_row = gate_ref[...].astype(jnp.float32)

    def gate_block(i, carry):
        rows = pl.ds(pl.multiple_of(i * 128, 128), 128)
        grad = (og[rows].astype(jnp.float32) * gate_row).astype(jnp.bfloat16)
        gpt[i] = grad.astype(jnp.float32).T.astype(jnp.bfloat16)
        return carry
    lax.fori_loop(0, TOK // 128, gate_block, 0)

    for r in range(1, NY):
        wy_wait(r)
    for r in range(1, NX):
        wx_copy(r).start()

    def attend(h):
        def body(it, carry):
            g = it // 2
            t = it % 2

            def qrow(i):
                return pl.ds(pl.multiple_of((t * GH + i) * (GW * TILE) + g * 96, 16), 96)

            def krow(i):
                return pl.ds(pl.multiple_of(i * (GW * TILE) + g * TILE, 16), 3 * TILE)

            queries = jnp.concatenate(
                [jnp.concatenate([qkv[h, 0, qrow(i)], bias[h, qrow(i)]], axis=1) for i in range(GH)], axis=0)
            keys = jnp.concatenate(
                [jnp.concatenate([qkv[h, 1, krow(i)], onehot[krow(i)]], axis=1) for i in range(GT * GH)], axis=0)
            values = jnp.concatenate([qkv[h, 2, krow(i)] for i in range(GT * GH)], axis=0)
            scores = lax.dot_general(
                queries, keys, (((1,), (1,)), ((), ())), preferred_element_type=jnp.float32)
            peak = jnp.max(scores, axis=1, keepdims=True)
            weights = jnp.exp2((scores - peak) * SCALE2)
            share = 1.0 / jnp.sum(weights, axis=1, keepdims=True)
            probs = (weights * share).astype(jnp.bfloat16)
            blended = jnp.dot(probs, values, preferred_element_type=jnp.float32).astype(jnp.bfloat16)
            for i in range(GH):
                att[2 * sq + h, qrow(i)] = blended[i * 96:(i + 1) * 96]
            return carry
        lax.fori_loop(0, 4, body, 0)

    def piece(z_from, core, h, half):
        return att.at[2 * sqi(z_from, core) + h, pl.ds(half * HALF, HALF)]

    def ag_direct(way, h, half):
        ref = piece(zh, c, h, half)
        step = 1 if way == 0 else -1
        return pltpu.make_async_remote_copy(
            ref, ref, agd_s.at[way, h, half], agd_r.at[way, h, half],
            device_id=(dp, sqi(zh + step, c)), device_id_type=MESH)

    def ag_direct_wait(way, h, half):
        ref = piece(zh - 1 if way == 0 else zh + 1, c, h, half)
        pltpu.make_async_remote_copy(
            ref, ref, agd_s.at[way, h, half], agd_r.at[way, h, half],
            device_id=(dp, sq), device_id_type=MESH).wait_recv()

    def ag_forward(h, half):
        ref = piece(zh - 1 if half == 0 else zh + 1, c, h, half)
        step = 1 if half == 0 else -1
        return pltpu.make_async_remote_copy(
            ref, ref, agf_s.at[h, half], agf_r.at[h, half],
            device_id=(dp, sqi(zh + step, c)), device_id_type=MESH)

    def ag_forward_wait(h, half):
        ref = piece(zh + 2, c, h, half)
        pltpu.make_async_remote_copy(
            ref, ref, agf_s.at[h, half], agf_r.at[h, half],
            device_id=(dp, sq), device_id_type=MESH).wait_recv()

    away = (0, -1, 1, 2)

    def ag_core(rel, h, half):
        ref = piece(zh + away[rel], c, h, half)
        return pltpu.make_async_remote_copy(
            ref, ref, agc_s.at[rel, h, half], agc_r.at[rel, h, half],
            device_id=(dp, zh * 2 + 1 - c), device_id_type=MESH)

    def ag_core_wait(rel):
        for h in range(2):
            for half in range(2):
                ref = piece(zh + away[rel], 1 - c, h, half)
                pltpu.make_async_remote_copy(
                    ref, ref, agc_s.at[rel, h, half], agc_r.at[rel, h, half],
                    device_id=(dp, sq), device_id_type=MESH).wait_recv()

    def send_own(h):
        ag_direct(0, h, 0).start()
        ag_direct(1, h, 1).start()
        ag_direct(0, h, 1).start()
        ag_direct(1, h, 0).start()
        ag_core(0, h, 0).start()
        ag_core(0, h, 1).start()

    def relay_direct(h):
        ag_direct_wait(0, h, 0)
        ag_forward(h, 0).start()
        ag_core(1, h, 0).start()
        ag_direct_wait(1, h, 1)
        ag_forward(h, 1).start()
        ag_core(2, h, 1).start()
        ag_direct_wait(0, h, 1)
        ag_core(1, h, 1).start()
        ag_direct_wait(1, h, 0)
        ag_core(2, h, 0).start()

    def relay_far(h):
        for half in range(2):
            ag_forward_wait(h, half)
            ag_core(3, h, half).start()

    def xs_copy(n, r):
        dest = lax.rem(x + r, NX)
        return pltpu.make_async_remote_copy(
            xs.at[n, pl.ds(pl.multiple_of(dest * 64, 64), 64)], xr.at[n, r],
            xs_sem.at[n, r], xr_sem.at[n, r],
            device_id=(dpi(y, dest, zl), sq), device_id_type=MESH)

    def grad_chunk(n, s):
        total = jnp.zeros((COLS, 256), jnp.float32)
        for i in range(TOK // 128):
            rows = pl.ds(i * 128, 128)
            part = jnp.concatenate([att[2 * s, rows], att[2 * s + 1, rows]], axis=1)
            total += jnp.dot(gpt[i], part, preferred_element_type=jnp.float32)
        turned = total.T
        gf[n] = turned
        xs[n] = turned.astype(jnp.bfloat16)
        for r in range(1, NX):
            xs_copy(n, r).start()

    def project_chunk(n, s):
        weight = wbuf[s].reshape(256, COLS)

        def body(i, carry):
            rows = pl.ds(pl.multiple_of(i * 288, 16), 288)
            part = jnp.concatenate([att[2 * s, rows], att[2 * s + 1, rows]], axis=1)
            value = jnp.dot(part, weight, preferred_element_type=jnp.float32)
            if n == 0:
                acc[rows] = value
            elif n < NS - 1:
                acc[rows] += value
            else:
                out_ref[rows] = ((acc[rows] + value) * gate_row).astype(jnp.bfloat16)
            return carry
        lax.fori_loop(0, TOK // 288, body, 0)

    def ys_copy(n, s):
        r = lax.rem(s + NY - y, NY)
        return pltpu.make_async_remote_copy(
            ys.at[n], yr.at[r], ys_sem.at[n], yr_sem.at[r],
            device_id=(dpi(s, x, zl), sq), device_id_type=MESH)

    def reduce_x(n, s):
        for r in range(1, NX):
            pltpu.make_async_remote_copy(
                xr.at[n, r], xr.at[n, r], xs_sem.at[n, r], xr_sem.at[n, r],
                device_id=(dp, sq), device_id_type=MESH).wait_recv()
        value = gf[n, pl.ds(pl.multiple_of(x * 64, 64), 64)]
        for r in range(1, NX):
            value += xr[n, r].astype(jnp.float32)
        ys[n] = value.astype(jnp.bfloat16)

        @pl.when(s == y)
        def _():
            yo[...] = value

        @pl.when(s != y)
        def _():
            ys_copy(n, s).start()

    chunk_of = [
        sqi(zh, c), sqi(zh, 1 - c), sqi(zh - 1, c), sqi(zh - 1, 1 - c),
        sqi(zh + 1, c), sqi(zh + 1, 1 - c), sqi(zh + 2, c), sqi(zh + 2, 1 - c),
    ]

    for h in range(2):
        for t in range(3):
            pltpu.make_async_copy(
                qkv.at[h, t, pl.ds(0, ROWS)], qkv.at[h, t, pl.ds(0, ROWS)], qr_sem.at[h, t, 0]).wait()

        def wait_one(r, carry, h=h):
            for t in range(3):
                qkv_wait(h, t, r)
            return carry
        lax.fori_loop(1, NS, wait_one, 0)
        attend(h)
        send_own(h)

    for r in range(1, NX):
        wx_wait(r)
    grad_chunk(0, chunk_of[0])
    project_chunk(0, chunk_of[0])
    relay_direct(0)
    ag_core_wait(0)
    grad_chunk(1, chunk_of[1])
    project_chunk(1, chunk_of[1])
    reduce_x(0, chunk_of[0])
    relay_direct(1)
    relay_far(0)
    reduce_x(1, chunk_of[1])
    grad_chunk(2, chunk_of[2])
    project_chunk(2, chunk_of[2])
    ag_core_wait(1)
    grad_chunk(3, chunk_of[3])
    project_chunk(3, chunk_of[3])
    reduce_x(2, chunk_of[2])
    grad_chunk(4, chunk_of[4])
    project_chunk(4, chunk_of[4])
    reduce_x(3, chunk_of[3])
    ag_core_wait(2)
    grad_chunk(5, chunk_of[5])
    project_chunk(5, chunk_of[5])
    relay_far(1)
    reduce_x(4, chunk_of[4])
    reduce_x(5, chunk_of[5])
    grad_chunk(6, chunk_of[6])
    ag_core_wait(3)
    grad_chunk(7, chunk_of[7])
    reduce_x(6, chunk_of[6])
    project_chunk(6, chunk_of[6])
    reduce_x(7, chunk_of[7])
    project_chunk(7, chunk_of[7])

    total = yo[...]
    for r in range(1, NY):
        pltpu.make_async_remote_copy(
            yr.at[r], yr.at[r], ys_sem.at[0], yr_sem.at[r],
            device_id=(dp, sq), device_id_type=MESH).wait_recv()
        total += yr[r].astype(jnp.float32)
    yo[...] = total
    zs[...] = yo[pl.ds(pl.multiple_of((1 - zl) * WROWS, 8), WROWS)]
    z_copy = pltpu.make_async_remote_copy(
        zs, zr, zs_sem.at[0], zs_sem.at[1],
        device_id=(dpi(y, x, 1 - zl), sq), device_id_type=MESH)
    z_copy.start()
    z_copy.wait_recv()
    wg_ref[...] = yo[pl.ds(pl.multiple_of(zl * WROWS, 8), WROWS)] + zr[...]

    z_copy.wait_send()
    w_z.wait_send()
    for h in range(2):
        def drain_one(r, carry, h=h):
            for t in range(3):
                qkv_copy(h, t, r).wait_send()
            return carry
        lax.fori_loop(1, NS, drain_one, 0)
    for r in range(1, NY):
        wy_copy(r).wait_send()
    for r in range(1, NX):
        wx_copy(r).wait_send()
    for h in range(2):
        for half in range(2):
            for way in range(2):
                ag_direct(way, h, half).wait_send()
            ag_forward(h, half).wait_send()
            for rel in range(4):
                ag_core(rel, h, half).wait_send()
    for n in range(NS):
        for r in range(1, NX):
            xs_copy(n, r).wait_send()

        @pl.when(chunk_of[n] != y)
        def _(n=n):
            ys_copy(n, chunk_of[n]).wait_send()


def per_device(query_rows, key_rows, value_rows, windows, out_weight, gate_scale, out_grad):
    anywhere = pl.BlockSpec(memory_space=pl.ANY)
    vmem = pl.BlockSpec(memory_space=pltpu.VMEM)
    smem = pl.BlockSpec(memory_space=pltpu.SMEM)
    bf16, f32 = jnp.bfloat16, jnp.float32
    dma = pltpu.SemaphoreType.DMA
    return pl.pallas_call(
        kernel,
        out_shape=(
            jax.ShapeDtypeStruct((TOK, COLS), bf16),
            jax.ShapeDtypeStruct((WROWS, COLS), f32),
        ),
        in_specs=[anywhere, anywhere, anywhere, smem, anywhere, vmem, anywhere],
        out_specs=(vmem, vmem),
        scratch_shapes=[
            pltpu.VMEM((2, 3, TOK, HEAD_DIM), bf16),
            pltpu.VMEM((TOK, 128), bf16),
            pltpu.VMEM((2, TOK, 128), bf16),
            pltpu.VMEM((2 * NS, TOK, HEAD_DIM), bf16),
            pltpu.VMEM((NY, NX, NZ, WROWS, COLS), bf16),
            pltpu.VMEM((TOK, COLS), bf16),
            pltpu.VMEM((TOK // 128, COLS, 128), bf16),
            pltpu.VMEM((TOK, COLS), f32),
            pltpu.VMEM((NS, 256, COLS), f32),
            pltpu.VMEM((NS, 256, COLS), bf16),
            pltpu.VMEM((NS, NX, 64, COLS), bf16),
            pltpu.VMEM((NS, 64, COLS), bf16),
            pltpu.VMEM((NY, 64, COLS), bf16),
            pltpu.VMEM((64, COLS), f32),
            pltpu.VMEM((WROWS, COLS), f32),
            pltpu.VMEM((WROWS, COLS), f32),
            dma((2, 3, NS)), dma((2, 3, NS)), dma((2,)), dma((2,)),
            dma((NY,)), dma((NY,)), dma((NX,)), dma((NX,)),
            dma((2, 2, 2)), dma((2, 2, 2)), dma((2, 2)), dma((2, 2)),
            dma((4, 2, 2)), dma((4, 2, 2)),
            dma((NS, NX)), dma((NS, NX)), dma((NS,)), dma((NY,)), dma((2,)),
        ],
        compiler_params=pltpu.CompilerParams(
            collective_id=0, has_side_effects=True, vmem_limit_bytes=56 * 1024 * 1024),
        name="video_attention_block",
    )(query_rows, key_rows, value_rows, windows, out_weight, gate_scale, out_grad)


def solution(mesh):
    return jax.shard_map(
        per_device,
        mesh=mesh,
        in_specs=(
            P(("dp", "seq"), None),
            P(("dp", "seq"), None),
            P(("dp", "seq"), None),
            P(),
            P("dp", "seq"),
            P("dp", "seq"),
            P("dp", "seq"),
        ),
        out_specs=(P("dp", "seq"), P("dp", "seq")),
        check_vma=False,
    )
```

```python
import math

import jax
import jax.numpy as jnp
from jax import lax
from jax.experimental import pallas as pl
from jax.experimental.pallas import tpu as pltpu
from jax.sharding import PartitionSpec as P

HEAD_DIM = 128
GT, GH, GW = 2, 3, 4
TILE = 48
NT = 24
TOK = 1152
ROWS = 144
NY, NX, NZ = 8, 4, 2
NZH = 4
NS = 8
COLS = 384
WROWS = 32
HALF = TOK // 2
HIDE = -(2.0**100)
MESH = pl.DeviceIdType.MESH
SCALE2 = math.log2(math.e) / math.sqrt(HEAD_DIM)


def kernel(
    q_ref, k_ref, v_ref, win_ref, w_ref, gate_ref, og_ref,
    out_ref, wg_ref,
    qkv, onehot, bias, att, wbuf, og, gpt, acc, turned, own, xs, xr, xf, xg, ys, yr, yo, zs, zr,
    qs_sem, qr_sem, loc_sem, wz_sem, wy_s, wy_r, wx_s, wx_r,
    agd_s, agd_r, agf_s, agf_r, agc_s, agc_r, xs_sem, xr_sem, xf_sem, xg_sem, ys_sem, yr_sem, zs_sem,
):
    dp = lax.axis_index("dp")
    sq = lax.axis_index("seq")
    zl = lax.rem(dp, NZ)
    x = lax.rem(dp // NZ, NX)
    y = dp // (NZ * NX)
    zh = sq // 2
    c = lax.rem(sq, 2)

    def dpi(yy, xx, zz):
        return (yy * NX + xx) * NZ + zz

    def sqi(zz, cc):
        return lax.rem(zz + 2 * NZH, NZH) * 2 + cc

    bar = pltpu.get_barrier_semaphore()

    def greet(device):
        pl.semaphore_signal(bar, 1, device_id=device, device_id_type=MESH)

    for r in range(1, NS):
        greet((dp, lax.rem(sq + r, NS)))
    for r in range(1, NX):
        greet((dpi(y, lax.rem(x + r, NX), zl), sq))
    for r in range(1, NY):
        greet((dpi(lax.rem(y + r, NY), x, zl), sq))
    greet((dpi(y, x, 1 - zl), sq))
    pl.semaphore_wait(bar, (NS - 1) + (NX - 1) + (NY - 1) + 1)

    w_local = pltpu.make_async_copy(w_ref, wbuf.at[y, x, zl], loc_sem.at[0])
    w_local.start()
    w_z = pltpu.make_async_remote_copy(
        w_ref, wbuf.at[y, x, zl], wz_sem.at[0], wz_sem.at[1],
        device_id=(dpi(y, x, 1 - zl), sq), device_id_type=MESH)
    w_z.start()
    og_copy = pltpu.make_async_copy(og_ref, og, loc_sem.at[1])
    og_copy.start()

    tensors = (q_ref, k_ref, v_ref)

    def qkv_copy(h, t, r):
        dest = lax.rem(sq + r, NS)
        src = tensors[t].at[:, pl.ds(pl.multiple_of(dest * 256 + h * 128, 128), 128)]
        return pltpu.make_async_remote_copy(
            src, qkv.at[h, t, pl.ds(pl.multiple_of(sq * ROWS, 16), ROWS)],
            qs_sem.at[h, t, r], qr_sem.at[h, t, r],
            device_id=(dp, dest), device_id_type=MESH)

    def qkv_own(h, t):
        src = tensors[t].at[:, pl.ds(pl.multiple_of(sq * 256 + h * 128, 128), 128)]
        return pltpu.make_async_copy(
            src, qkv.at[h, t, pl.ds(pl.multiple_of(sq * ROWS, 16), ROWS)], qr_sem.at[h, t, 0])

    def qkv_wait(h, t, r):
        source = lax.rem(sq + NS - r, NS)
        land = qkv.at[h, t, pl.ds(pl.multiple_of(source * ROWS, 16), ROWS)]
        pltpu.make_async_remote_copy(
            land, land, qs_sem.at[h, t, r], qr_sem.at[h, t, r],
            device_id=(dp, source), device_id_type=MESH).wait_recv()

    def qkv_start(h, t):
        def start_one(r, carry):
            qkv_copy(h, t, r).start()
            return carry
        lax.fori_loop(1, NS, start_one, 0)
        qkv_own(h, t).start()

    def qkv_sent(h, t):
        def drain_one(r, carry):
            qkv_copy(h, t, r).wait_send()
            return carry
        lax.fori_loop(1, NS, drain_one, 0)

    for t in range(3):
        qkv_start(0, t)
    for t in range(3):
        qkv_start(1, t)

    lane = lax.broadcasted_iota(jnp.int32, (TOK, 128), 1)
    tile = lax.broadcasted_iota(jnp.int32, (TOK, 128), 0) // TILE
    onehot[...] = jnp.where(lane == tile, 1.0, 0.0).astype(jnp.bfloat16)
    limits = (GT, GH, GW)
    q_at = (tile // (GH * GW), tile // GW % GH, tile % GW)
    k_at = (lane // (GH * GW), lane // GW % GH, lane % GW)
    for h in range(2):
        inside = lane < NT
        for d in range(3):
            extent = jnp.minimum(win_ref[d, 2 * sq + h], limits[d])
            first = jnp.clip(q_at[d] - (extent - 1) // 2, 0, limits[d] - extent)
            inside = inside & (k_at[d] >= first) & (k_at[d] < first + extent)
        bias[h] = jnp.where(inside | (lane >= NT), 0.0, HIDE).astype(jnp.bfloat16)

    w_local.wait()
    w_z.wait_recv()

    def wy_copy(r):
        dest = lax.rem(y + r, NY)
        return pltpu.make_async_remote_copy(
            wbuf.at[y, x], wbuf.at[y, x], wy_s.at[r], wy_r.at[r],
            device_id=(dpi(dest, x, zl), sq), device_id_type=MESH)

    def wy_wait(r):
        land = wbuf.at[lax.rem(y + NY - r, NY), x]
        pltpu.make_async_remote_copy(
            land, land, wy_s.at[r], wy_r.at[r],
            device_id=(dpi(y, x, zl), sq), device_id_type=MESH).wait_recv()

    def wx_copy(r):
        dest = lax.rem(x + r, NX)
        return pltpu.make_async_remote_copy(
            wbuf.at[:, x], wbuf.at[:, x], wx_s.at[r], wx_r.at[r],
            device_id=(dpi(y, dest, zl), sq), device_id_type=MESH)

    def wx_wait(r):
        land = wbuf.at[:, lax.rem(x + NX - r, NX)]
        pltpu.make_async_remote_copy(
            land, land, wx_s.at[r], wx_r.at[r],
            device_id=(dpi(y, x, zl), sq), device_id_type=MESH).wait_recv()

    for r in range(1, NY):
        wy_copy(r).start()

    og_copy.wait()
    gate_row = gate_ref[...].astype(jnp.float32)

    def gate_block(i, carry):
        rows = pl.ds(pl.multiple_of(i * 128, 128), 128)
        grad = (og[rows].astype(jnp.float32) * gate_row).astype(jnp.bfloat16)
        gpt[i] = grad.astype(jnp.float32).T.astype(jnp.bfloat16)
        return carry
    lax.fori_loop(0, TOK // 128, gate_block, 0)

    for r in range(1, NY):
        wy_wait(r)
    for r in range(1, NX):
        wx_copy(r).start()

    def attend(h):
        def body(it, carry):
            g = it // 2
            t = it % 2

            def qrow(i):
                return pl.ds(pl.multiple_of((t * GH + i) * (GW * TILE) + g * 96, 16), 96)

            def krow(i):
                return pl.ds(pl.multiple_of(i * (GW * TILE) + g * TILE, 16), 3 * TILE)

            queries = jnp.concatenate(
                [jnp.concatenate([qkv[h, 0, qrow(i)], bias[h, qrow(i)]], axis=1) for i in range(GH)], axis=0)
            keys = jnp.concatenate(
                [jnp.concatenate([qkv[h, 1, krow(i)], onehot[krow(i)]], axis=1) for i in range(GT * GH)], axis=0)
            values = jnp.concatenate([qkv[h, 2, krow(i)] for i in range(GT * GH)], axis=0)
            scores = lax.dot_general(
                queries, keys, (((1,), (1,)), ((), ())), preferred_element_type=jnp.float32)
            peak = jnp.max(scores, axis=1, keepdims=True)
            weights = jnp.exp2((scores - peak) * SCALE2)
            share = 1.0 / jnp.sum(weights, axis=1, keepdims=True)
            probs = (weights * share).astype(jnp.bfloat16)
            blended = jnp.dot(probs, values, preferred_element_type=jnp.float32).astype(jnp.bfloat16)
            for i in range(GH):
                att[2 * sq + h, qrow(i)] = blended[i * 96:(i + 1) * 96]
            return carry
        lax.fori_loop(0, 4, body, 0)

    def piece(z_from, core, h, half):
        return att.at[2 * sqi(z_from, core) + h, pl.ds(half * HALF, HALF)]

    def ag_direct(way, h, half):
        ref = piece(zh, c, h, half)
        step = 1 if way == 0 else -1
        return pltpu.make_async_remote_copy(
            ref, ref, agd_s.at[way, h, half], agd_r.at[way, h, half],
            device_id=(dp, sqi(zh + step, c)), device_id_type=MESH)

    def ag_direct_wait(way, h, half):
        ref = piece(zh - 1 if way == 0 else zh + 1, c, h, half)
        pltpu.make_async_remote_copy(
            ref, ref, agd_s.at[way, h, half], agd_r.at[way, h, half],
            device_id=(dp, sq), device_id_type=MESH).wait_recv()

    def ag_forward(h, half):
        ref = piece(zh - 1 if half == 0 else zh + 1, c, h, half)
        step = 1 if half == 0 else -1
        return pltpu.make_async_remote_copy(
            ref, ref, agf_s.at[h, half], agf_r.at[h, half],
            device_id=(dp, sqi(zh + step, c)), device_id_type=MESH)

    def ag_forward_wait(h, half):
        ref = piece(zh + 2, c, h, half)
        pltpu.make_async_remote_copy(
            ref, ref, agf_s.at[h, half], agf_r.at[h, half],
            device_id=(dp, sq), device_id_type=MESH).wait_recv()

    away = (0, -1, 1, 2)

    def ag_core(rel, h, half):
        ref = piece(zh + away[rel], c, h, half)
        return pltpu.make_async_remote_copy(
            ref, ref, agc_s.at[rel, h, half], agc_r.at[rel, h, half],
            device_id=(dp, zh * 2 + 1 - c), device_id_type=MESH)

    def ag_core_wait(rel, h):
        for half in range(2):
            ref = piece(zh + away[rel], 1 - c, h, half)
            pltpu.make_async_remote_copy(
                ref, ref, agc_s.at[rel, h, half], agc_r.at[rel, h, half],
                device_id=(dp, sq), device_id_type=MESH).wait_recv()

    def send_own(h):
        ag_direct(0, h, 0).start()
        ag_direct(1, h, 1).start()
        ag_direct(0, h, 1).start()
        ag_direct(1, h, 0).start()
        ag_core(0, h, 0).start()
        ag_core(0, h, 1).start()

    def relay_first(h):
        ag_direct_wait(0, h, 0)
        ag_forward(h, 0).start()
        ag_core(1, h, 0).start()
        ag_direct_wait(1, h, 1)
        ag_forward(h, 1).start()
        ag_core(2, h, 1).start()

    def relay_second(h):
        ag_direct_wait(0, h, 1)
        ag_core(1, h, 1).start()
        ag_direct_wait(1, h, 0)
        ag_core(2, h, 0).start()

    def relay_far(h):
        for half in range(2):
            ag_forward_wait(h, half)
            ag_core(3, h, half).start()

    chunk_of = [
        sqi(zh, c), sqi(zh, 1 - c), sqi(zh - 1, c), sqi(zh - 1, 1 - c),
        sqi(zh + 1, c), sqi(zh + 1, 1 - c), sqi(zh + 2, c), sqi(zh + 2, 1 - c),
    ]

    partner = x + 1 - 2 * lax.rem(x, 2)

    def xs_copy(n, h):
        return pltpu.make_async_remote_copy(
            xs.at[n, h], xr.at[n, h], xs_sem.at[n, h], xr_sem.at[n, h],
            device_id=(dpi(y, partner, zl), sq), device_id_type=MESH)

    def xf_copy(n):
        return pltpu.make_async_remote_copy(
            xf.at[n], xg.at[n], xf_sem.at[n], xg_sem.at[n],
            device_id=(dpi(y, NX - 1 - x, zl), sq), device_id_type=MESH)

    def head_rows(pair, rows):
        return jnp.concatenate([att[2 * chunk_of[n] + h, rows] for n, h in pair], axis=1)

    def grad_pair(pair):
        total = jnp.zeros((COLS, 256), jnp.float32)
        for i in range(TOK // 128):
            total += jnp.dot(gpt[i], head_rows(pair, pl.ds(i * 128, 128)), preferred_element_type=jnp.float32)
        turned[...] = total.T
        for i, (n, h) in enumerate(pair):
            kept = lax.rem(x // 2 + h + x, 2)
            own[n, h] = turned[pl.ds(pl.multiple_of(i * 128 + kept * 64, 64), 64)]
            xs[n, h] = turned[pl.ds(pl.multiple_of(i * 128 + (1 - kept) * 64, 64), 64)].astype(jnp.bfloat16)
            xs_copy(n, h).start()

    def project_pair(pair, first=False, last=False):
        weight = jnp.concatenate(
            [wbuf[chunk_of[n], 2 * h:2 * h + 2].reshape(128, COLS) for n, h in pair], axis=0)

        def body(i, carry):
            rows = pl.ds(pl.multiple_of(i * 288, 16), 288)
            value = jnp.dot(head_rows(pair, rows), weight, preferred_element_type=jnp.float32)
            if first:
                acc[rows] = value
            elif last:
                out_ref[rows] = ((acc[rows] + value) * gate_row).astype(jnp.bfloat16)
            else:
                acc[rows] += value
            return carry
        lax.fori_loop(0, TOK // 288, body, 0)

    def ys_copy(n):
        s = chunk_of[n]
        r = lax.rem(s + NY - y, NY)
        return pltpu.make_async_remote_copy(
            ys.at[n], yr.at[r], ys_sem.at[n], yr_sem.at[r],
            device_id=(dpi(s, x, zl), sq), device_id_type=MESH)

    def near_sum(n, h):
        xs_copy(n, h).wait_recv()
        return own[n, h] + xr[n, h].astype(jnp.float32)

    def middle_pair(pair):
        for n, h in pair:
            @pl.when(x // 2 != h)
            def _(n=n, h=h):
                xf[n] = near_sum(n, h).astype(jnp.bfloat16)
                xf_copy(n).start()

    def reduce_pair(pair):
        for n, h in pair:
            @pl.when(x // 2 == h)
            def _(n=n, h=h):
                near = near_sum(n, h)
                xf_copy(n).wait_recv()
                value = near + xg[n].astype(jnp.float32)
                ys[n] = value.astype(jnp.bfloat16)

                @pl.when(chunk_of[n] == y)
                def _():
                    yo[...] = value

                @pl.when(chunk_of[n] != y)
                def _():
                    ys_copy(n).start()

    def drain_pair(pair):
        for n, h in pair:
            xs_copy(n, h).wait_send()

            @pl.when(x // 2 != h)
            def _(n=n):
                xf_copy(n).wait_send()

    def drain_ag(h):
        for half in range(2):
            for way in range(2):
                ag_direct(way, h, half).wait_send()
            ag_forward(h, half).wait_send()
            for rel in range(4):
                ag_core(rel, h, half).wait_send()

    def qkv_arrive(h):
        for t in range(3):
            pltpu.make_async_copy(
                qkv.at[h, t, pl.ds(0, ROWS)], qkv.at[h, t, pl.ds(0, ROWS)], qr_sem.at[h, t, 0]).wait()

        def wait_one(r, carry):
            for t in range(3):
                qkv_wait(h, t, r)
            return carry
        lax.fori_loop(1, NS, wait_one, 0)

    pair_a, pair_b = ((0, 0), (0, 1)), ((1, 0), (1, 1))
    pair_c, pair_d, pair_e = ((2, 0), (3, 0)), ((4, 0), (5, 0)), ((6, 0), (7, 0))
    pair_f, pair_g, pair_h = ((2, 1), (3, 1)), ((4, 1), (5, 1)), ((6, 1), (7, 1))

    qkv_arrive(0)
    attend(0)
    send_own(0)
    qkv_arrive(1)
    relay_first(0)
    attend(1)
    send_own(1)
    for r in range(1, NX):
        wx_wait(r)
    grad_pair(pair_a)
    project_pair(pair_a, first=True)
    relay_second(0)
    for h in range(2):
        ag_core_wait(0, h)
    grad_pair(pair_b)
    project_pair(pair_b)
    middle_pair(pair_a)
    ag_core_wait(1, 0)
    grad_pair(pair_c)
    project_pair(pair_c)
    middle_pair(pair_b)
    ag_core_wait(2, 0)
    grad_pair(pair_d)
    project_pair(pair_d)
    reduce_pair(pair_a)
    middle_pair(pair_c)
    relay_far(0)
    relay_first(1)
    w_z.wait_send()
    for r in range(1, NY):
        wy_copy(r).wait_send()
    for r in range(1, NX):
        wx_copy(r).wait_send()
    for h in range(2):
        for t in range(3):
            qkv_sent(h, t)
    ag_core_wait(3, 0)
    grad_pair(pair_e)
    project_pair(pair_e)
    reduce_pair(pair_b)
    middle_pair(pair_d)
    relay_second(1)
    reduce_pair(pair_c)
    middle_pair(pair_e)
    ag_core_wait(1, 1)
    grad_pair(pair_f)
    ag_core_wait(2, 1)
    grad_pair(pair_g)
    project_pair(pair_f)
    middle_pair(pair_f)
    project_pair(pair_g)
    middle_pair(pair_g)
    reduce_pair(pair_d)
    reduce_pair(pair_e)
    drain_ag(0)
    for pair in (pair_a, pair_b, pair_c, pair_d, pair_e):
        drain_pair(pair)
    relay_far(1)
    reduce_pair(pair_f)
    reduce_pair(pair_g)
    ag_core_wait(3, 1)
    grad_pair(pair_h)
    project_pair(pair_h, last=True)
    middle_pair(pair_h)
    drain_pair(pair_f)
    drain_pair(pair_g)
    drain_ag(1)
    reduce_pair(pair_h)

    total = yo[...]
    for r in range(1, NY):
        pltpu.make_async_remote_copy(
            yr.at[r], yr.at[r], ys_sem.at[0], yr_sem.at[r],
            device_id=(dp, sq), device_id_type=MESH).wait_recv()
        total += yr[r].astype(jnp.float32)
    yo[...] = total
    zs[...] = yo[pl.ds(pl.multiple_of((1 - zl) * WROWS, 8), WROWS)]
    z_copy = pltpu.make_async_remote_copy(
        zs, zr, zs_sem.at[0], zs_sem.at[1],
        device_id=(dpi(y, x, 1 - zl), sq), device_id_type=MESH)
    z_copy.start()
    z_copy.wait_recv()
    wg_ref[...] = yo[pl.ds(pl.multiple_of(zl * WROWS, 8), WROWS)] + zr[...]

    z_copy.wait_send()
    drain_pair(pair_h)
    for n in range(NS):
        @pl.when(chunk_of[n] != y)
        def _(n=n):
            ys_copy(n).wait_send()


def per_device(query_rows, key_rows, value_rows, windows, out_weight, gate_scale, out_grad):
    anywhere = pl.BlockSpec(memory_space=pl.ANY)
    vmem = pl.BlockSpec(memory_space=pltpu.VMEM)
    smem = pl.BlockSpec(memory_space=pltpu.SMEM)
    bf16, f32 = jnp.bfloat16, jnp.float32
    dma = pltpu.SemaphoreType.DMA
    return pl.pallas_call(
        kernel,
        out_shape=(
            jax.ShapeDtypeStruct((TOK, COLS), bf16),
            jax.ShapeDtypeStruct((WROWS, COLS), f32),
        ),
        in_specs=[anywhere, anywhere, anywhere, smem, anywhere, vmem, anywhere],
        out_specs=(vmem, vmem),
        scratch_shapes=[
            pltpu.VMEM((2, 3, TOK, HEAD_DIM), bf16),
            pltpu.VMEM((TOK, 128), bf16),
            pltpu.VMEM((2, TOK, 128), bf16),
            pltpu.VMEM((2 * NS, TOK, HEAD_DIM), bf16),
            pltpu.VMEM((NY, NX, NZ, WROWS, COLS), bf16),
            pltpu.VMEM((TOK, COLS), bf16),
            pltpu.VMEM((TOK // 128, COLS, 128), bf16),
            pltpu.VMEM((TOK, COLS), f32),
            pltpu.VMEM((256, COLS), f32),
            pltpu.VMEM((NS, 2, 64, COLS), f32),
            pltpu.VMEM((NS, 2, 64, COLS), bf16),
            pltpu.VMEM((NS, 2, 64, COLS), bf16),
            pltpu.VMEM((NS, 64, COLS), bf16),
            pltpu.VMEM((NS, 64, COLS), bf16),
            pltpu.VMEM((NS, 64, COLS), bf16),
            pltpu.VMEM((NY, 64, COLS), bf16),
            pltpu.VMEM((64, COLS), f32),
            pltpu.VMEM((WROWS, COLS), f32),
            pltpu.VMEM((WROWS, COLS), f32),
            dma((2, 3, NS)), dma((2, 3, NS)), dma((2,)), dma((2,)),
            dma((NY,)), dma((NY,)), dma((NX,)), dma((NX,)),
            dma((2, 2, 2)), dma((2, 2, 2)), dma((2, 2)), dma((2, 2)),
            dma((4, 2, 2)), dma((4, 2, 2)),
            dma((NS, 2)), dma((NS, 2)), dma((NS,)), dma((NS,)), dma((NS,)), dma((NY,)), dma((2,)),
        ],
        compiler_params=pltpu.CompilerParams(
            collective_id=0, has_side_effects=True, vmem_limit_bytes=56 * 1024 * 1024),
        name="video_attention_block",
    )(query_rows, key_rows, value_rows, windows.T, out_weight, gate_scale, out_grad)


def solution(mesh):
    return jax.shard_map(
        per_device,
        mesh=mesh,
        in_specs=(
            P(("dp", "seq"), None),
            P(("dp", "seq"), None),
            P(("dp", "seq"), None),
            P(),
            P("dp", "seq"),
            P("dp", "seq"),
            P("dp", "seq"),
        ),
        out_specs=(P("dp", "seq"), P("dp", "seq")),
        check_vma=False,
    )
```

```python
import math

import jax
import jax.numpy as jnp
from jax import lax
from jax.experimental import pallas as pl
from jax.experimental.pallas import tpu as pltpu
from jax.sharding import PartitionSpec as P

HEAD_DIM = 128
GT, GH, GW = 2, 3, 4
TILE = 48
NT = 24
TOK = 1152
ROWS = 144
NY, NX, NZ = 8, 4, 2
NZH = 4
NS = 8
COLS = 384
WROWS = 32
HALF = TOK // 2
HIDE = -(2.0**100)
MESH = pl.DeviceIdType.MESH
SCALE2 = math.log2(math.e) / math.sqrt(HEAD_DIM)


def kernel(
    q_ref, k_ref, v_ref, win_ref, w_ref, gate_ref, og_ref,
    out_ref, wg_ref,
    qkv, onehot, bias, att, wbuf, og, gpt, acc, turned, own, xs, xr, xf, xg, ys, yr, yo, zs, zr,
    qs_sem, qr_sem, loc_sem, wz_sem, wy_s, wy_r, wx_s, wx_r,
    agd_s, agd_r, agf_s, agf_r, agc_s, agc_r, xs_sem, xr_sem, xf_sem, xg_sem, ys_sem, yr_sem, zs_sem,
):
    dp = lax.axis_index("dp")
    sq = lax.axis_index("seq")
    zl = lax.rem(dp, NZ)
    x = lax.rem(dp // NZ, NX)
    y = dp // (NZ * NX)
    zh = sq // 2
    c = lax.rem(sq, 2)

    def dpi(yy, xx, zz):
        return (yy * NX + xx) * NZ + zz

    def sqi(zz, cc):
        return lax.rem(zz + 2 * NZH, NZH) * 2 + cc

    bar = pltpu.get_barrier_semaphore()

    def greet(device):
        pl.semaphore_signal(bar, 1, device_id=device, device_id_type=MESH)

    for r in range(1, NS):
        greet((dp, lax.rem(sq + r, NS)))
    for r in range(1, NX):
        greet((dpi(y, lax.rem(x + r, NX), zl), sq))
    for r in range(1, NY):
        greet((dpi(lax.rem(y + r, NY), x, zl), sq))
    greet((dpi(y, x, 1 - zl), sq))
    pl.semaphore_wait(bar, (NS - 1) + (NX - 1) + (NY - 1) + 1)

    w_local = pltpu.make_async_copy(w_ref, wbuf.at[y, x, zl], loc_sem.at[0])
    w_local.start()
    w_z = pltpu.make_async_remote_copy(
        w_ref, wbuf.at[y, x, zl], wz_sem.at[0], wz_sem.at[1],
        device_id=(dpi(y, x, 1 - zl), sq), device_id_type=MESH)
    w_z.start()
    og_copy = pltpu.make_async_copy(og_ref, og, loc_sem.at[1])
    og_copy.start()

    tensors = (q_ref, k_ref, v_ref)

    def qkv_copy(h, t, r):
        dest = lax.rem(sq + r, NS)
        src = tensors[t].at[:, pl.ds(pl.multiple_of(dest * 256 + h * 128, 128), 128)]
        return pltpu.make_async_remote_copy(
            src, qkv.at[h, t, pl.ds(pl.multiple_of(sq * ROWS, 16), ROWS)],
            qs_sem.at[h, t, r], qr_sem.at[h, t, r],
            device_id=(dp, dest), device_id_type=MESH)

    def qkv_own(h, t):
        src = tensors[t].at[:, pl.ds(pl.multiple_of(sq * 256 + h * 128, 128), 128)]
        return pltpu.make_async_copy(
            src, qkv.at[h, t, pl.ds(pl.multiple_of(sq * ROWS, 16), ROWS)], qr_sem.at[h, t, 0])

    def qkv_wait(h, t, r):
        source = lax.rem(sq + NS - r, NS)
        land = qkv.at[h, t, pl.ds(pl.multiple_of(source * ROWS, 16), ROWS)]
        pltpu.make_async_remote_copy(
            land, land, qs_sem.at[h, t, r], qr_sem.at[h, t, r],
            device_id=(dp, source), device_id_type=MESH).wait_recv()

    def qkv_start(h, t):
        def start_one(r, carry):
            qkv_copy(h, t, r).start()
            return carry
        lax.fori_loop(1, NS, start_one, 0)
        qkv_own(h, t).start()

    def qkv_sent(h, t):
        def drain_one(r, carry):
            qkv_copy(h, t, r).wait_send()
            return carry
        lax.fori_loop(1, NS, drain_one, 0)

    for t in range(3):
        qkv_start(0, t)
    qkv_start(1, 0)

    lane = lax.broadcasted_iota(jnp.int32, (TOK, 128), 1)
    tile = lax.broadcasted_iota(jnp.int32, (TOK, 128), 0) // TILE
    onehot[...] = jnp.where(lane == tile, 1.0, 0.0).astype(jnp.bfloat16)
    limits = (GT, GH, GW)
    q_at = (tile // (GH * GW), tile // GW % GH, tile % GW)
    k_at = (lane // (GH * GW), lane // GW % GH, lane % GW)
    for h in range(2):
        inside = lane < NT
        for d in range(3):
            extent = jnp.minimum(win_ref[d, 2 * sq + h], limits[d])
            first = jnp.clip(q_at[d] - (extent - 1) // 2, 0, limits[d] - extent)
            inside = inside & (k_at[d] >= first) & (k_at[d] < first + extent)
        bias[h] = jnp.where(inside | (lane >= NT), 0.0, HIDE).astype(jnp.bfloat16)

    w_local.wait()
    w_z.wait_recv()

    def wy_copy(r):
        dest = lax.rem(y + r, NY)
        return pltpu.make_async_remote_copy(
            wbuf.at[y, x], wbuf.at[y, x], wy_s.at[r], wy_r.at[r],
            device_id=(dpi(dest, x, zl), sq), device_id_type=MESH)

    def wy_wait(r):
        land = wbuf.at[lax.rem(y + NY - r, NY), x]
        pltpu.make_async_remote_copy(
            land, land, wy_s.at[r], wy_r.at[r],
            device_id=(dpi(y, x, zl), sq), device_id_type=MESH).wait_recv()

    def wx_copy(r):
        dest = lax.rem(x + r, NX)
        return pltpu.make_async_remote_copy(
            wbuf.at[:, x], wbuf.at[:, x], wx_s.at[r], wx_r.at[r],
            device_id=(dpi(y, dest, zl), sq), device_id_type=MESH)

    def wx_wait(r):
        land = wbuf.at[:, lax.rem(x + NX - r, NX)]
        pltpu.make_async_remote_copy(
            land, land, wx_s.at[r], wx_r.at[r],
            device_id=(dpi(y, x, zl), sq), device_id_type=MESH).wait_recv()

    for r in range(1, NY):
        wy_copy(r).start()

    og_copy.wait()
    gate_row = gate_ref[...].astype(jnp.float32)

    def gate_block(i, carry):
        rows = pl.ds(pl.multiple_of(i * 128, 128), 128)
        grad = (og[rows].astype(jnp.float32) * gate_row).astype(jnp.bfloat16)
        gpt[i] = grad.astype(jnp.float32).T.astype(jnp.bfloat16)
        return carry
    lax.fori_loop(0, TOK // 128, gate_block, 0)

    for r in range(1, NY):
        wy_wait(r)
    for r in range(1, NX):
        wx_copy(r).start()
    qkv_sent(0, 0)
    qkv_start(1, 1)
    qkv_start(1, 2)

    def attend(h):
        def body(it, carry):
            g = it // 2
            t = it % 2

            def qrow(i):
                return pl.ds(pl.multiple_of((t * GH + i) * (GW * TILE) + g * 96, 16), 96)

            def krow(i):
                return pl.ds(pl.multiple_of(i * (GW * TILE) + g * TILE, 16), 3 * TILE)

            queries = jnp.concatenate(
                [jnp.concatenate([qkv[h, 0, qrow(i)], bias[h, qrow(i)]], axis=1) for i in range(GH)], axis=0)
            keys = jnp.concatenate(
                [jnp.concatenate([qkv[h, 1, krow(i)], onehot[krow(i)]], axis=1) for i in range(GT * GH)], axis=0)
            values = jnp.concatenate([qkv[h, 2, krow(i)] for i in range(GT * GH)], axis=0)
            scores = lax.dot_general(
                queries, keys, (((1,), (1,)), ((), ())), preferred_element_type=jnp.float32)
            peak = jnp.max(scores, axis=1, keepdims=True)
            weights = jnp.exp2((scores - peak) * SCALE2)
            share = 1.0 / jnp.sum(weights, axis=1, keepdims=True)
            probs = (weights * share).astype(jnp.bfloat16)
            blended = jnp.dot(probs, values, preferred_element_type=jnp.float32).astype(jnp.bfloat16)
            for i in range(GH):
                att[2 * sq + h, qrow(i)] = blended[i * 96:(i + 1) * 96]
            return carry
        lax.fori_loop(0, 4, body, 0)

    def piece(z_from, core, h, half):
        return att.at[2 * sqi(z_from, core) + h, pl.ds(half * HALF, HALF)]

    def ag_direct(way, h, half):
        ref = piece(zh, c, h, half)
        step = 1 if way == 0 else -1
        return pltpu.make_async_remote_copy(
            ref, ref, agd_s.at[way, h, half], agd_r.at[way, h, half],
            device_id=(dp, sqi(zh + step, c)), device_id_type=MESH)

    def ag_direct_wait(way, h, half):
        ref = piece(zh - 1 if way == 0 else zh + 1, c, h, half)
        pltpu.make_async_remote_copy(
            ref, ref, agd_s.at[way, h, half], agd_r.at[way, h, half],
            device_id=(dp, sq), device_id_type=MESH).wait_recv()

    def ag_forward(h, half):
        ref = piece(zh - 1 if half == 0 else zh + 1, c, h, half)
        step = 1 if half == 0 else -1
        return pltpu.make_async_remote_copy(
            ref, ref, agf_s.at[h, half], agf_r.at[h, half],
            device_id=(dp, sqi(zh + step, c)), device_id_type=MESH)

    def ag_forward_wait(h, half):
        ref = piece(zh + 2, c, h, half)
        pltpu.make_async_remote_copy(
            ref, ref, agf_s.at[h, half], agf_r.at[h, half],
            device_id=(dp, sq), device_id_type=MESH).wait_recv()

    away = (0, -1, 1, 2)

    def ag_core(rel, h, half):
        ref = piece(zh + away[rel], c, h, half)
        return pltpu.make_async_remote_copy(
            ref, ref, agc_s.at[rel, h, half], agc_r.at[rel, h, half],
            device_id=(dp, zh * 2 + 1 - c), device_id_type=MESH)

    def ag_core_wait(rel, h):
        for half in range(2):
            ref = piece(zh + away[rel], 1 - c, h, half)
            pltpu.make_async_remote_copy(
                ref, ref, agc_s.at[rel, h, half], agc_r.at[rel, h, half],
                device_id=(dp, sq), device_id_type=MESH).wait_recv()

    def send_own(h):
        ag_direct(0, h, 0).start()
        ag_direct(1, h, 1).start()
        ag_direct(0, h, 1).start()
        ag_direct(1, h, 0).start()
        ag_core(0, h, 0).start()
        ag_core(0, h, 1).start()

    def relay_first(h):
        ag_direct_wait(0, h, 0)
        ag_forward(h, 0).start()
        ag_core(1, h, 0).start()
        ag_direct_wait(1, h, 1)
        ag_forward(h, 1).start()
        ag_core(2, h, 1).start()

    def relay_second(h):
        ag_direct_wait(0, h, 1)
        ag_core(1, h, 1).start()
        ag_direct_wait(1, h, 0)
        ag_core(2, h, 0).start()

    def relay_far(h):
        for half in range(2):
            ag_forward_wait(h, half)
            ag_core(3, h, half).start()

    chunk_of = [
        sqi(zh, c), sqi(zh, 1 - c), sqi(zh - 1, c), sqi(zh - 1, 1 - c),
        sqi(zh + 1, c), sqi(zh + 1, 1 - c), sqi(zh + 2, c), sqi(zh + 2, 1 - c),
    ]

    partner = x + 1 - 2 * lax.rem(x, 2)

    def xs_copy(n, h):
        return pltpu.make_async_remote_copy(
            xs.at[n, h], xr.at[n, h], xs_sem.at[n, h], xr_sem.at[n, h],
            device_id=(dpi(y, partner, zl), sq), device_id_type=MESH)

    def xf_copy(n):
        return pltpu.make_async_remote_copy(
            xf.at[n], xg.at[n], xf_sem.at[n], xg_sem.at[n],
            device_id=(dpi(y, NX - 1 - x, zl), sq), device_id_type=MESH)

    def head_rows(pair, rows):
        return jnp.concatenate([att[2 * chunk_of[n] + h, rows] for n, h in pair], axis=1)

    def grad_pair(pair):
        total = jnp.zeros((COLS, 256), jnp.float32)
        for i in range(TOK // 128):
            total += jnp.dot(gpt[i], head_rows(pair, pl.ds(i * 128, 128)), preferred_element_type=jnp.float32)
        turned[...] = total.T
        for i, (n, h) in enumerate(pair):
            kept = lax.rem(x // 2 + h + x, 2)
            own[n, h] = turned[pl.ds(pl.multiple_of(i * 128 + kept * 64, 64), 64)]
            xs[n, h] = turned[pl.ds(pl.multiple_of(i * 128 + (1 - kept) * 64, 64), 64)].astype(jnp.bfloat16)
            xs_copy(n, h).start()

    def project_pair(pair, first=False, last=False):
        weight = jnp.concatenate(
            [wbuf[chunk_of[n], 2 * h:2 * h + 2].reshape(128, COLS) for n, h in pair], axis=0)

        def body(i, carry):
            rows = pl.ds(pl.multiple_of(i * 288, 16), 288)
            value = jnp.dot(head_rows(pair, rows), weight, preferred_element_type=jnp.float32)
            if first:
                acc[rows] = value
            elif last:
                out_ref[rows] = ((acc[rows] + value) * gate_row).astype(jnp.bfloat16)
            else:
                acc[rows] += value
            return carry
        lax.fori_loop(0, TOK // 288, body, 0)

    def ys_copy(n):
        s = chunk_of[n]
        r = lax.rem(s + NY - y, NY)
        return pltpu.make_async_remote_copy(
            ys.at[n], yr.at[r], ys_sem.at[n], yr_sem.at[r],
            device_id=(dpi(s, x, zl), sq), device_id_type=MESH)

    def near_sum(n, h):
        xs_copy(n, h).wait_recv()
        return own[n, h] + xr[n, h].astype(jnp.float32)

    def middle_pair(pair):
        for n, h in pair:
            @pl.when(x // 2 != h)
            def _(n=n, h=h):
                xf[n] = near_sum(n, h).astype(jnp.bfloat16)
                xf_copy(n).start()

    def reduce_pair(pair):
        for n, h in pair:
            @pl.when(x // 2 == h)
            def _(n=n, h=h):
                near = near_sum(n, h)
                xf_copy(n).wait_recv()
                value = near + xg[n].astype(jnp.float32)
                ys[n] = value.astype(jnp.bfloat16)

                @pl.when(chunk_of[n] == y)
                def _():
                    yo[...] = value

                @pl.when(chunk_of[n] != y)
                def _():
                    ys_copy(n).start()

    def drain_pair(pair):
        for n, h in pair:
            xs_copy(n, h).wait_send()

            @pl.when(x // 2 != h)
            def _(n=n):
                xf_copy(n).wait_send()

    def drain_ag(h):
        for half in range(2):
            for way in range(2):
                ag_direct(way, h, half).wait_send()
            ag_forward(h, half).wait_send()
            for rel in range(4):
                ag_core(rel, h, half).wait_send()

    def qkv_arrive(h):
        for t in range(3):
            pltpu.make_async_copy(
                qkv.at[h, t, pl.ds(0, ROWS)], qkv.at[h, t, pl.ds(0, ROWS)], qr_sem.at[h, t, 0]).wait()

        def wait_one(r, carry):
            for t in range(3):
                qkv_wait(h, t, r)
            return carry
        lax.fori_loop(1, NS, wait_one, 0)

    pair_a, pair_b = ((0, 0), (0, 1)), ((1, 0), (1, 1))
    pair_c, pair_d, pair_e = ((2, 0), (3, 0)), ((4, 0), (5, 0)), ((6, 0), (7, 0))
    pair_f, pair_g, pair_h = ((2, 1), (3, 1)), ((4, 1), (5, 1)), ((6, 1), (7, 1))

    qkv_arrive(0)
    attend(0)
    send_own(0)
    qkv_arrive(1)
    relay_first(0)
    attend(1)
    send_own(1)
    for r in range(1, NX):
        wx_wait(r)
    grad_pair(pair_a)
    project_pair(pair_a, first=True)
    relay_second(0)
    for h in range(2):
        ag_core_wait(0, h)
    grad_pair(pair_b)
    project_pair(pair_b)
    middle_pair(pair_a)
    ag_core_wait(1, 0)
    grad_pair(pair_c)
    project_pair(pair_c)
    middle_pair(pair_b)
    ag_core_wait(2, 0)
    grad_pair(pair_d)
    project_pair(pair_d)
    reduce_pair(pair_a)
    middle_pair(pair_c)
    relay_far(0)
    relay_first(1)
    w_z.wait_send()
    for r in range(1, NY):
        wy_copy(r).wait_send()
    for r in range(1, NX):
        wx_copy(r).wait_send()
    qkv_sent(0, 1)
    qkv_sent(0, 2)
    qkv_sent(1, 0)
    qkv_sent(1, 1)
    qkv_sent(1, 2)
    ag_core_wait(3, 0)
    grad_pair(pair_e)
    project_pair(pair_e)
    reduce_pair(pair_b)
    middle_pair(pair_d)
    relay_second(1)
    reduce_pair(pair_c)
    middle_pair(pair_e)
    ag_core_wait(1, 1)
    grad_pair(pair_f)
    ag_core_wait(2, 1)
    grad_pair(pair_g)
    project_pair(pair_f)
    middle_pair(pair_f)
    project_pair(pair_g)
    middle_pair(pair_g)
    reduce_pair(pair_d)
    reduce_pair(pair_e)
    drain_ag(0)
    for pair in (pair_a, pair_b, pair_c, pair_d, pair_e):
        drain_pair(pair)
    relay_far(1)
    reduce_pair(pair_f)
    reduce_pair(pair_g)
    ag_core_wait(3, 1)
    grad_pair(pair_h)
    project_pair(pair_h, last=True)
    middle_pair(pair_h)
    drain_pair(pair_f)
    drain_pair(pair_g)
    drain_ag(1)
    reduce_pair(pair_h)

    total = yo[...]
    for r in range(1, NY):
        pltpu.make_async_remote_copy(
            yr.at[r], yr.at[r], ys_sem.at[0], yr_sem.at[r],
            device_id=(dp, sq), device_id_type=MESH).wait_recv()
        total += yr[r].astype(jnp.float32)
    yo[...] = total
    zs[...] = yo[pl.ds(pl.multiple_of((1 - zl) * WROWS, 8), WROWS)]
    z_copy = pltpu.make_async_remote_copy(
        zs, zr, zs_sem.at[0], zs_sem.at[1],
        device_id=(dpi(y, x, 1 - zl), sq), device_id_type=MESH)
    z_copy.start()
    z_copy.wait_recv()
    wg_ref[...] = yo[pl.ds(pl.multiple_of(zl * WROWS, 8), WROWS)] + zr[...]

    z_copy.wait_send()
    drain_pair(pair_h)
    for n in range(NS):
        @pl.when(chunk_of[n] != y)
        def _(n=n):
            ys_copy(n).wait_send()


def per_device(query_rows, key_rows, value_rows, windows, out_weight, gate_scale, out_grad):
    anywhere = pl.BlockSpec(memory_space=pl.ANY)
    vmem = pl.BlockSpec(memory_space=pltpu.VMEM)
    smem = pl.BlockSpec(memory_space=pltpu.SMEM)
    bf16, f32 = jnp.bfloat16, jnp.float32
    dma = pltpu.SemaphoreType.DMA
    return pl.pallas_call(
        kernel,
        out_shape=(
            pltpu.VMEM((TOK, COLS), bf16),
            pltpu.VMEM((WROWS, COLS), f32),
        ),
        in_specs=[anywhere, anywhere, anywhere, smem, anywhere, vmem, anywhere],
        out_specs=(vmem, vmem),
        scratch_shapes=[
            pltpu.VMEM((2, 3, TOK, HEAD_DIM), bf16),
            pltpu.VMEM((TOK, 128), bf16),
            pltpu.VMEM((2, TOK, 128), bf16),
            pltpu.VMEM((2 * NS, TOK, HEAD_DIM), bf16),
            pltpu.VMEM((NY, NX, NZ, WROWS, COLS), bf16),
            pltpu.VMEM((TOK, COLS), bf16),
            pltpu.VMEM((TOK // 128, COLS, 128), bf16),
            pltpu.VMEM((TOK, COLS), f32),
            pltpu.VMEM((256, COLS), f32),
            pltpu.VMEM((NS, 2, 64, COLS), f32),
            pltpu.VMEM((NS, 2, 64, COLS), bf16),
            pltpu.VMEM((NS, 2, 64, COLS), bf16),
            pltpu.VMEM((NS, 64, COLS), bf16),
            pltpu.VMEM((NS, 64, COLS), bf16),
            pltpu.VMEM((NS, 64, COLS), bf16),
            pltpu.VMEM((NY, 64, COLS), bf16),
            pltpu.VMEM((64, COLS), f32),
            pltpu.VMEM((WROWS, COLS), f32),
            pltpu.VMEM((WROWS, COLS), f32),
            dma((2, 3, NS)), dma((2, 3, NS)), dma((2,)), dma((2,)),
            dma((NY,)), dma((NY,)), dma((NX,)), dma((NX,)),
            dma((2, 2, 2)), dma((2, 2, 2)), dma((2, 2)), dma((2, 2)),
            dma((4, 2, 2)), dma((4, 2, 2)),
            dma((NS, 2)), dma((NS, 2)), dma((NS,)), dma((NS,)), dma((NS,)), dma((NY,)), dma((2,)),
        ],
        compiler_params=pltpu.CompilerParams(
            collective_id=0, has_side_effects=True, vmem_limit_bytes=56 * 1024 * 1024),
        name="video_attention_block",
    )(query_rows, key_rows, value_rows, windows.T, out_weight, gate_scale, out_grad)


def solution(mesh):
    return jax.shard_map(
        per_device,
        mesh=mesh,
        in_specs=(
            P(("dp", "seq"), None),
            P(("dp", "seq"), None),
            P(("dp", "seq"), None),
            P(),
            P("dp", "seq"),
            P("dp", "seq"),
            P("dp", "seq"),
        ),
        out_specs=(P("dp", "seq"), P("dp", "seq")),
        check_vma=False,
    )
```

```python
import math

import jax
import jax.numpy as jnp
from jax import lax
from jax.experimental import pallas as pl
from jax.experimental.pallas import tpu as pltpu
from jax.sharding import PartitionSpec as P

HEAD_DIM = 128
GT, GH, GW = 2, 3, 4
TILE = 48
NT = 24
TOK = 1152
ROWS = 144
NY, NX, NZ = 8, 4, 2
NZH = 4
NS = 8
COLS = 384
WROWS = 32
HALF = TOK // 2
HIDE = -(2.0**100)
MESH = pl.DeviceIdType.MESH
SCALE2 = math.log2(math.e) / math.sqrt(HEAD_DIM)


def kernel(
    q_ref, k_ref, v_ref, win_ref, w_ref, gate_ref, og_ref,
    out_ref, wg_ref,
    qkv, onehot, bias, att, wbuf, og, gpt, acc, turned, own, xs, xr, xf, xg, ys, yr, yo, total,
    qs_sem, qr_sem, loc_sem, wz_sem, wy_s, wy_r, wx_s, wx_r,
    agd_s, agd_r, agf_s, agf_r, agc_s, agc_r, xs_sem, xr_sem, xf_sem, xg_sem, ys_sem, yr_sem,
):
    dp = lax.axis_index("dp")
    sq = lax.axis_index("seq")
    zl = lax.rem(dp, NZ)
    x = lax.rem(dp // NZ, NX)
    y = dp // (NZ * NX)
    zh = sq // 2
    c = lax.rem(sq, 2)

    def dpi(yy, xx, zz):
        return (yy * NX + xx) * NZ + zz

    def sqi(zz, cc):
        return lax.rem(zz + 2 * NZH, NZH) * 2 + cc

    bar = pltpu.get_barrier_semaphore()

    def greet(device):
        pl.semaphore_signal(bar, 1, device_id=device, device_id_type=MESH)

    for r in range(1, NS):
        greet((dp, lax.rem(sq + r, NS)))
    for r in range(1, NX):
        greet((dpi(y, lax.rem(x + r, NX), zl), sq))
    for r in range(1, NY):
        greet((dpi(lax.rem(y + r, NY), x, zl), sq))
    for r in range(NY):
        greet((dpi(lax.rem(y + r, NY), x, 1 - zl), sq))
    pl.semaphore_wait(bar, (NS - 1) + (NX - 1) + (NY - 1) + NY)

    w_local = pltpu.make_async_copy(w_ref, wbuf.at[y, x, zl], loc_sem.at[0])
    w_local.start()
    w_z = pltpu.make_async_remote_copy(
        w_ref, wbuf.at[y, x, zl], wz_sem.at[0], wz_sem.at[1],
        device_id=(dpi(y, x, 1 - zl), sq), device_id_type=MESH)
    w_z.start()
    og_copy = pltpu.make_async_copy(og_ref, og, loc_sem.at[1])
    og_copy.start()

    tensors = (q_ref, k_ref, v_ref)

    def qkv_copy(h, t, r):
        dest = lax.rem(sq + r, NS)
        src = tensors[t].at[:, pl.ds(pl.multiple_of(dest * 256 + h * 128, 128), 128)]
        return pltpu.make_async_remote_copy(
            src, qkv.at[h, t, pl.ds(pl.multiple_of(sq * ROWS, 16), ROWS)],
            qs_sem.at[h, t, r], qr_sem.at[h, t, r],
            device_id=(dp, dest), device_id_type=MESH)

    def qkv_own(h, t):
        src = tensors[t].at[:, pl.ds(pl.multiple_of(sq * 256 + h * 128, 128), 128)]
        return pltpu.make_async_copy(
            src, qkv.at[h, t, pl.ds(pl.multiple_of(sq * ROWS, 16), ROWS)], qr_sem.at[h, t, 0])

    def qkv_wait(h, t, r):
        source = lax.rem(sq + NS - r, NS)
        land = qkv.at[h, t, pl.ds(pl.multiple_of(source * ROWS, 16), ROWS)]
        pltpu.make_async_remote_copy(
            land, land, qs_sem.at[h, t, r], qr_sem.at[h, t, r],
            device_id=(dp, source), device_id_type=MESH).wait_recv()

    def qkv_start(h, t):
        def start_one(r, carry):
            qkv_copy(h, t, r).start()
            return carry
        lax.fori_loop(1, NS, start_one, 0)
        qkv_own(h, t).start()

    def qkv_sent(h, t):
        def drain_one(r, carry):
            qkv_copy(h, t, r).wait_send()
            return carry
        lax.fori_loop(1, NS, drain_one, 0)

    for t in range(3):
        qkv_start(0, t)
    qkv_start(1, 0)

    lane = lax.broadcasted_iota(jnp.int32, (TOK, 128), 1)
    tile = lax.broadcasted_iota(jnp.int32, (TOK, 128), 0) // TILE
    onehot[...] = jnp.where(lane == tile, 1.0, 0.0).astype(jnp.bfloat16)
    limits = (GT, GH, GW)
    q_at = (tile // (GH * GW), tile // GW % GH, tile % GW)
    k_at = (lane // (GH * GW), lane // GW % GH, lane % GW)
    for h in range(2):
        inside = lane < NT
        for d in range(3):
            extent = jnp.minimum(win_ref[d, 2 * sq + h], limits[d])
            first = jnp.clip(q_at[d] - (extent - 1) // 2, 0, limits[d] - extent)
            inside = inside & (k_at[d] >= first) & (k_at[d] < first + extent)
        bias[h] = jnp.where(inside | (lane >= NT), 0.0, HIDE).astype(jnp.bfloat16)

    w_local.wait()
    w_z.wait_recv()

    def wy_copy(r):
        dest = lax.rem(y + r, NY)
        return pltpu.make_async_remote_copy(
            wbuf.at[y, x], wbuf.at[y, x], wy_s.at[r], wy_r.at[r],
            device_id=(dpi(dest, x, zl), sq), device_id_type=MESH)

    def wy_wait(r):
        land = wbuf.at[lax.rem(y + NY - r, NY), x]
        pltpu.make_async_remote_copy(
            land, land, wy_s.at[r], wy_r.at[r],
            device_id=(dpi(y, x, zl), sq), device_id_type=MESH).wait_recv()

    def wx_copy(r):
        dest = lax.rem(x + r, NX)
        return pltpu.make_async_remote_copy(
            wbuf.at[:, x], wbuf.at[:, x], wx_s.at[r], wx_r.at[r],
            device_id=(dpi(y, dest, zl), sq), device_id_type=MESH)

    def wx_wait(r):
        land = wbuf.at[:, lax.rem(x + NX - r, NX)]
        pltpu.make_async_remote_copy(
            land, land, wx_s.at[r], wx_r.at[r],
            device_id=(dpi(y, x, zl), sq), device_id_type=MESH).wait_recv()

    for r in range(1, NY):
        wy_copy(r).start()

    og_copy.wait()
    gate_row = gate_ref[...].astype(jnp.float32)

    def gate_block(i, carry):
        rows = pl.ds(pl.multiple_of(i * 128, 128), 128)
        grad = (og[rows].astype(jnp.float32) * gate_row).astype(jnp.bfloat16)
        gpt[i] = grad.astype(jnp.float32).T.astype(jnp.bfloat16)
        return carry
    lax.fori_loop(0, TOK // 128, gate_block, 0)

    for r in range(1, NY):
        wy_wait(r)
    for r in range(1, NX):
        wx_copy(r).start()
    qkv_sent(0, 0)
    qkv_start(1, 1)
    qkv_start(1, 2)

    def attend(h):
        def body(it, carry):
            g = it // 2
            t = it % 2

            def qrow(i):
                return pl.ds(pl.multiple_of((t * GH + i) * (GW * TILE) + g * 96, 16), 96)

            def krow(i):
                return pl.ds(pl.multiple_of(i * (GW * TILE) + g * TILE, 16), 3 * TILE)

            queries = jnp.concatenate(
                [jnp.concatenate([qkv[h, 0, qrow(i)], bias[h, qrow(i)]], axis=1) for i in range(GH)], axis=0)
            keys = jnp.concatenate(
                [jnp.concatenate([qkv[h, 1, krow(i)], onehot[krow(i)]], axis=1) for i in range(GT * GH)], axis=0)
            values = jnp.concatenate([qkv[h, 2, krow(i)] for i in range(GT * GH)], axis=0)
            scores = lax.dot_general(
                queries, keys, (((1,), (1,)), ((), ())), preferred_element_type=jnp.float32)
            peak = jnp.max(scores, axis=1, keepdims=True)
            weights = jnp.exp2((scores - peak) * SCALE2)
            share = 1.0 / jnp.sum(weights, axis=1, keepdims=True)
            probs = (weights * share).astype(jnp.bfloat16)
            blended = jnp.dot(probs, values, preferred_element_type=jnp.float32).astype(jnp.bfloat16)
            for i in range(GH):
                att[2 * sq + h, qrow(i)] = blended[i * 96:(i + 1) * 96]
            return carry
        lax.fori_loop(0, 4, body, 0)

    def piece(z_from, core, h, half):
        return att.at[2 * sqi(z_from, core) + h, pl.ds(half * HALF, HALF)]

    def ag_direct(way, h, half):
        ref = piece(zh, c, h, half)
        step = 1 if way == 0 else -1
        return pltpu.make_async_remote_copy(
            ref, ref, agd_s.at[way, h, half], agd_r.at[way, h, half],
            device_id=(dp, sqi(zh + step, c)), device_id_type=MESH)

    def ag_direct_wait(way, h, half):
        ref = piece(zh - 1 if way == 0 else zh + 1, c, h, half)
        pltpu.make_async_remote_copy(
            ref, ref, agd_s.at[way, h, half], agd_r.at[way, h, half],
            device_id=(dp, sq), device_id_type=MESH).wait_recv()

    def ag_forward(h, half):
        ref = piece(zh - 1 if half == 0 else zh + 1, c, h, half)
        step = 1 if half == 0 else -1
        return pltpu.make_async_remote_copy(
            ref, ref, agf_s.at[h, half], agf_r.at[h, half],
            device_id=(dp, sqi(zh + step, c)), device_id_type=MESH)

    def ag_forward_wait(h, half):
        ref = piece(zh + 2, c, h, half)
        pltpu.make_async_remote_copy(
            ref, ref, agf_s.at[h, half], agf_r.at[h, half],
            device_id=(dp, sq), device_id_type=MESH).wait_recv()

    away = (0, -1, 1, 2)

    def ag_core(rel, h, half):
        ref = piece(zh + away[rel], c, h, half)
        return pltpu.make_async_remote_copy(
            ref, ref, agc_s.at[rel, h, half], agc_r.at[rel, h, half],
            device_id=(dp, zh * 2 + 1 - c), device_id_type=MESH)

    def ag_core_wait(rel, h):
        for half in range(2):
            ref = piece(zh + away[rel], 1 - c, h, half)
            pltpu.make_async_remote_copy(
                ref, ref, agc_s.at[rel, h, half], agc_r.at[rel, h, half],
                device_id=(dp, sq), device_id_type=MESH).wait_recv()

    def send_own(h):
        ag_direct(0, h, 0).start()
        ag_direct(1, h, 1).start()
        ag_direct(0, h, 1).start()
        ag_direct(1, h, 0).start()
        ag_core(0, h, 0).start()
        ag_core(0, h, 1).start()

    def relay_first(h):
        ag_direct_wait(0, h, 0)
        ag_forward(h, 0).start()
        ag_core(1, h, 0).start()
        ag_direct_wait(1, h, 1)
        ag_forward(h, 1).start()
        ag_core(2, h, 1).start()

    def relay_second(h):
        ag_direct_wait(0, h, 1)
        ag_core(1, h, 1).start()
        ag_direct_wait(1, h, 0)
        ag_core(2, h, 0).start()

    def relay_far(h):
        for half in range(2):
            ag_forward_wait(h, half)
            ag_core(3, h, half).start()

    chunk_of = [
        sqi(zh, c), sqi(zh, 1 - c), sqi(zh - 1, c), sqi(zh - 1, 1 - c),
        sqi(zh + 1, c), sqi(zh + 1, 1 - c), sqi(zh + 2, c), sqi(zh + 2, 1 - c),
    ]

    partner = x + 1 - 2 * lax.rem(x, 2)

    def xs_copy(n, h):
        return pltpu.make_async_remote_copy(
            xs.at[n, h], xr.at[n, h], xs_sem.at[n, h], xr_sem.at[n, h],
            device_id=(dpi(y, partner, zl), sq), device_id_type=MESH)

    def xf_copy(n):
        return pltpu.make_async_remote_copy(
            xf.at[n], xg.at[n], xf_sem.at[n], xg_sem.at[n],
            device_id=(dpi(y, NX - 1 - x, zl), sq), device_id_type=MESH)

    def head_rows(pair, rows):
        return jnp.concatenate([att[2 * chunk_of[n] + h, rows] for n, h in pair], axis=1)

    def grad_pair(pair):
        total = jnp.zeros((COLS, 256), jnp.float32)
        for i in range(TOK // 128):
            total += jnp.dot(gpt[i], head_rows(pair, pl.ds(i * 128, 128)), preferred_element_type=jnp.float32)
        turned[...] = total.T
        for i, (n, h) in enumerate(pair):
            kept = lax.rem(x // 2 + h + x, 2)
            own[n, h] = turned[pl.ds(pl.multiple_of(i * 128 + kept * 64, 64), 64)]
            xs[n, h] = turned[pl.ds(pl.multiple_of(i * 128 + (1 - kept) * 64, 64), 64)].astype(jnp.bfloat16)
            xs_copy(n, h).start()

    def project_pair(pair, first=False, last=False):
        weight = jnp.concatenate(
            [wbuf[chunk_of[n], 2 * h:2 * h + 2].reshape(128, COLS) for n, h in pair], axis=0)

        def body(i, carry):
            rows = pl.ds(pl.multiple_of(i * 288, 16), 288)
            value = jnp.dot(head_rows(pair, rows), weight, preferred_element_type=jnp.float32)
            if first:
                acc[rows] = value
            elif last:
                out_ref[rows] = ((acc[rows] + value) * gate_row).astype(jnp.bfloat16)
            else:
                acc[rows] += value
            return carry
        lax.fori_loop(0, TOK // 288, body, 0)

    def ys_copy(n, side):
        s = chunk_of[n]
        r = lax.rem(s + NY - y, NY)
        target = zl if side == 0 else 1 - zl
        return pltpu.make_async_remote_copy(
            ys.at[n, side], yr.at[side, r], ys_sem.at[n, side], yr_sem.at[side, r],
            device_id=(dpi(s, x, target), sq), device_id_type=MESH)

    def near_sum(n, h):
        xs_copy(n, h).wait_recv()
        return own[n, h] + xr[n, h].astype(jnp.float32)

    def middle_pair(pair):
        for n, h in pair:
            @pl.when(x // 2 != h)
            def _(n=n, h=h):
                xf[n] = near_sum(n, h).astype(jnp.bfloat16)
                xf_copy(n).start()

    def reduce_pair(pair):
        for n, h in pair:
            @pl.when(x // 2 == h)
            def _(n=n, h=h):
                near = near_sum(n, h)
                xf_copy(n).wait_recv()
                total[...] = near + xg[n].astype(jnp.float32)
                mine = total[pl.ds(pl.multiple_of(zl * WROWS, 8), WROWS)]
                ys[n, 1] = total[pl.ds(pl.multiple_of((1 - zl) * WROWS, 8), WROWS)].astype(jnp.bfloat16)
                ys_copy(n, 1).start()

                @pl.when(chunk_of[n] == y)
                def _():
                    yo[...] = mine

                @pl.when(chunk_of[n] != y)
                def _():
                    ys[n, 0] = mine.astype(jnp.bfloat16)
                    ys_copy(n, 0).start()

    def drain_pair(pair):
        for n, h in pair:
            xs_copy(n, h).wait_send()

            @pl.when(x // 2 != h)
            def _(n=n):
                xf_copy(n).wait_send()

    def drain_ag(h):
        for half in range(2):
            for way in range(2):
                ag_direct(way, h, half).wait_send()
            ag_forward(h, half).wait_send()
            for rel in range(4):
                ag_core(rel, h, half).wait_send()

    def qkv_arrive(h):
        for t in range(3):
            pltpu.make_async_copy(
                qkv.at[h, t, pl.ds(0, ROWS)], qkv.at[h, t, pl.ds(0, ROWS)], qr_sem.at[h, t, 0]).wait()

        def wait_one(r, carry):
            for t in range(3):
                qkv_wait(h, t, r)
            return carry
        lax.fori_loop(1, NS, wait_one, 0)

    pair_a, pair_b = ((0, 0), (0, 1)), ((1, 0), (1, 1))
    pair_c, pair_d, pair_e = ((2, 0), (3, 0)), ((4, 0), (5, 0)), ((6, 0), (7, 0))
    pair_f, pair_g, pair_h = ((2, 1), (3, 1)), ((4, 1), (5, 1)), ((6, 1), (7, 1))

    qkv_arrive(0)
    attend(0)
    send_own(0)
    qkv_arrive(1)
    relay_first(0)
    attend(1)
    send_own(1)
    for r in range(1, NX):
        wx_wait(r)
    grad_pair(pair_a)
    project_pair(pair_a, first=True)
    relay_second(0)
    for h in range(2):
        ag_core_wait(0, h)
    grad_pair(pair_b)
    project_pair(pair_b)
    middle_pair(pair_a)
    ag_core_wait(1, 0)
    grad_pair(pair_c)
    project_pair(pair_c)
    middle_pair(pair_b)
    ag_core_wait(2, 0)
    grad_pair(pair_d)
    project_pair(pair_d)
    middle_pair(pair_c)
    relay_far(0)
    relay_first(1)
    w_z.wait_send()
    for r in range(1, NY):
        wy_copy(r).wait_send()
    for r in range(1, NX):
        wx_copy(r).wait_send()
    qkv_sent(0, 1)
    qkv_sent(0, 2)
    qkv_sent(1, 0)
    qkv_sent(1, 1)
    qkv_sent(1, 2)
    ag_core_wait(3, 0)
    grad_pair(pair_e)
    project_pair(pair_e)
    middle_pair(pair_d)
    relay_second(1)
    middle_pair(pair_e)
    ag_core_wait(1, 1)
    grad_pair(pair_f)
    ag_core_wait(2, 1)
    grad_pair(pair_g)
    project_pair(pair_f)
    middle_pair(pair_f)
    project_pair(pair_g)
    middle_pair(pair_g)
    drain_ag(0)
    for pair in (pair_a, pair_b, pair_c, pair_d, pair_e):
        drain_pair(pair)
    relay_far(1)
    reduce_pair(pair_a)
    reduce_pair(pair_b)
    reduce_pair(pair_c)
    reduce_pair(pair_d)
    reduce_pair(pair_e)
    ag_core_wait(3, 1)
    grad_pair(pair_h)
    reduce_pair(pair_f)
    reduce_pair(pair_g)
    middle_pair(pair_h)
    project_pair(pair_h, last=True)
    drain_pair(pair_f)
    drain_pair(pair_g)
    drain_ag(1)
    reduce_pair(pair_h)

    summed = yo[...]
    for side in range(2):
        for r in range(1 - side, NY):
            pltpu.make_async_remote_copy(
                yr.at[side, r], yr.at[side, r], ys_sem.at[0, 0], yr_sem.at[side, r],
                device_id=(dp, sq), device_id_type=MESH).wait_recv()
            summed += yr[side, r].astype(jnp.float32)
    wg_ref[...] = summed

    drain_pair(pair_h)
    for n in range(NS):
        ys_copy(n, 1).wait_send()

        @pl.when(chunk_of[n] != y)
        def _(n=n):
            ys_copy(n, 0).wait_send()


def per_device(query_rows, key_rows, value_rows, windows, out_weight, gate_scale, out_grad):
    anywhere = pl.BlockSpec(memory_space=pl.ANY)
    vmem = pl.BlockSpec(memory_space=pltpu.VMEM)
    smem = pl.BlockSpec(memory_space=pltpu.SMEM)
    bf16, f32 = jnp.bfloat16, jnp.float32
    dma = pltpu.SemaphoreType.DMA
    return pl.pallas_call(
        kernel,
        out_shape=(
            pltpu.VMEM((TOK, COLS), bf16),
            pltpu.VMEM((WROWS, COLS), f32),
        ),
        in_specs=[anywhere, anywhere, anywhere, smem, anywhere, vmem, anywhere],
        out_specs=(vmem, vmem),
        scratch_shapes=[
            pltpu.VMEM((2, 3, TOK, HEAD_DIM), bf16),
            pltpu.VMEM((TOK, 128), bf16),
            pltpu.VMEM((2, TOK, 128), bf16),
            pltpu.VMEM((2 * NS, TOK, HEAD_DIM), bf16),
            pltpu.VMEM((NY, NX, NZ, WROWS, COLS), bf16),
            pltpu.VMEM((TOK, COLS), bf16),
            pltpu.VMEM((TOK // 128, COLS, 128), bf16),
            pltpu.VMEM((TOK, COLS), f32),
            pltpu.VMEM((256, COLS), f32),
            pltpu.VMEM((NS, 2, 64, COLS), f32),
            pltpu.VMEM((NS, 2, 64, COLS), bf16),
            pltpu.VMEM((NS, 2, 64, COLS), bf16),
            pltpu.VMEM((NS, 64, COLS), bf16),
            pltpu.VMEM((NS, 64, COLS), bf16),
            pltpu.VMEM((NS, 2, WROWS, COLS), bf16),
            pltpu.VMEM((2, NY, WROWS, COLS), bf16),
            pltpu.VMEM((WROWS, COLS), f32),
            pltpu.VMEM((64, COLS), f32),
            dma((2, 3, NS)), dma((2, 3, NS)), dma((2,)), dma((2,)),
            dma((NY,)), dma((NY,)), dma((NX,)), dma((NX,)),
            dma((2, 2, 2)), dma((2, 2, 2)), dma((2, 2)), dma((2, 2)),
            dma((4, 2, 2)), dma((4, 2, 2)),
            dma((NS, 2)), dma((NS, 2)), dma((NS,)), dma((NS,)), dma((NS, 2)), dma((2, NY)),
        ],
        compiler_params=pltpu.CompilerParams(
            collective_id=0, has_side_effects=True, vmem_limit_bytes=56 * 1024 * 1024),
        name="video_attention_block",
    )(query_rows, key_rows, value_rows, windows.T, out_weight, gate_scale, out_grad)


def solution(mesh):
    return jax.shard_map(
        per_device,
        mesh=mesh,
        in_specs=(
            P(("dp", "seq"), None),
            P(("dp", "seq"), None),
            P(("dp", "seq"), None),
            P(),
            P("dp", "seq"),
            P("dp", "seq"),
            P("dp", "seq"),
        ),
        out_specs=(P("dp", "seq"), P("dp", "seq")),
        check_vma=False,
    )
```

```python
import math

import jax
import jax.numpy as jnp
from jax import lax
from jax.experimental import pallas as pl
from jax.experimental.pallas import tpu as pltpu
from jax.sharding import PartitionSpec as P

HEAD_DIM = 128
GT, GH, GW = 2, 3, 4
TILE = 48
NT = 24
TOK = 1152
ROWS = 144
NY, NX, NZ = 8, 4, 2
NZH = 4
NS = 8
COLS = 384
WROWS = 32
HALF = TOK // 2
HIDE = -(2.0**100)
MESH = pl.DeviceIdType.MESH
SCALE2 = math.log2(math.e) / math.sqrt(HEAD_DIM)


def kernel(
    q_ref, k_ref, v_ref, win_ref, w_ref, gate_ref, og_ref,
    out_ref, wg_ref,
    qkv, onehot, bias, att, wbuf, og, gpt, acc, turned, own, xs, xr, xf, xg, ys, yr, yo, total,
    qs_sem, qr_sem, loc_sem, wz_sem, wy_s, wy_r, wx_s, wx_r,
    agd_s, agd_r, agf_s, agf_r, agc_s, agc_r, xs_sem, xr_sem, xf_sem, xg_sem, ys_sem, yr_sem,
):
    dp = lax.axis_index("dp")
    sq = lax.axis_index("seq")
    zl = lax.rem(dp, NZ)
    x = lax.rem(dp // NZ, NX)
    y = dp // (NZ * NX)
    zh = sq // 2
    c = lax.rem(sq, 2)

    def dpi(yy, xx, zz):
        return (yy * NX + xx) * NZ + zz

    def sqi(zz, cc):
        return lax.rem(zz + 2 * NZH, NZH) * 2 + cc

    bar = pltpu.get_barrier_semaphore()

    def greet(device):
        pl.semaphore_signal(bar, 1, device_id=device, device_id_type=MESH)

    for r in range(1, NS):
        greet((dp, lax.rem(sq + r, NS)))
    for r in range(1, NX):
        greet((dpi(y, lax.rem(x + r, NX), zl), sq))
    for r in range(1, NY):
        greet((dpi(lax.rem(y + r, NY), x, zl), sq))
    for r in range(NY):
        greet((dpi(lax.rem(y + r, NY), x, 1 - zl), sq))
    pl.semaphore_wait(bar, (NS - 1) + (NX - 1) + (NY - 1) + NY)

    w_local = pltpu.make_async_copy(w_ref, wbuf.at[y, x, zl], loc_sem.at[0])
    w_local.start()
    w_z = pltpu.make_async_remote_copy(
        w_ref, wbuf.at[y, x, zl], wz_sem.at[0], wz_sem.at[1],
        device_id=(dpi(y, x, 1 - zl), sq), device_id_type=MESH)
    w_z.start()
    og_copy = pltpu.make_async_copy(og_ref, og, loc_sem.at[1])
    og_copy.start()

    tensors = (q_ref, k_ref, v_ref)

    def qkv_copy(h, t, r):
        dest = lax.rem(sq + r, NS)
        src = tensors[t].at[:, pl.ds(pl.multiple_of(dest * 256 + h * 128, 128), 128)]
        return pltpu.make_async_remote_copy(
            src, qkv.at[h, t, pl.ds(pl.multiple_of(sq * ROWS, 16), ROWS)],
            qs_sem.at[h, t, r], qr_sem.at[h, t, r],
            device_id=(dp, dest), device_id_type=MESH)

    def qkv_own(h, t):
        src = tensors[t].at[:, pl.ds(pl.multiple_of(sq * 256 + h * 128, 128), 128)]
        return pltpu.make_async_copy(
            src, qkv.at[h, t, pl.ds(pl.multiple_of(sq * ROWS, 16), ROWS)], qr_sem.at[h, t, 0])

    def qkv_wait(h, t, r):
        source = lax.rem(sq + NS - r, NS)
        land = qkv.at[h, t, pl.ds(pl.multiple_of(source * ROWS, 16), ROWS)]
        pltpu.make_async_remote_copy(
            land, land, qs_sem.at[h, t, r], qr_sem.at[h, t, r],
            device_id=(dp, source), device_id_type=MESH).wait_recv()

    def qkv_start(h, t):
        def start_one(r, carry):
            qkv_copy(h, t, r).start()
            return carry
        lax.fori_loop(1, NS, start_one, 0)
        qkv_own(h, t).start()

    def qkv_sent(h, t):
        def drain_one(r, carry):
            qkv_copy(h, t, r).wait_send()
            return carry
        lax.fori_loop(1, NS, drain_one, 0)

    for t in range(3):
        qkv_start(0, t)
    qkv_start(1, 0)

    lane = lax.broadcasted_iota(jnp.int32, (TOK, 128), 1)
    tile = lax.broadcasted_iota(jnp.int32, (TOK, 128), 0) // TILE
    onehot[...] = jnp.where(lane == tile, 1.0, 0.0).astype(jnp.bfloat16)
    limits = (GT, GH, GW)
    q_at = (tile // (GH * GW), tile // GW % GH, tile % GW)
    k_at = (lane // (GH * GW), lane // GW % GH, lane % GW)
    for h in range(2):
        inside = lane < NT
        for d in range(3):
            extent = jnp.minimum(win_ref[d, 2 * sq + h], limits[d])
            first = jnp.clip(q_at[d] - (extent - 1) // 2, 0, limits[d] - extent)
            inside = inside & (k_at[d] >= first) & (k_at[d] < first + extent)
        bias[h] = jnp.where(inside | (lane >= NT), 0.0, HIDE).astype(jnp.bfloat16)

    w_local.wait()
    w_z.wait_recv()

    def wy_copy(r):
        dest = lax.rem(y + r, NY)
        return pltpu.make_async_remote_copy(
            wbuf.at[y, x], wbuf.at[y, x], wy_s.at[r], wy_r.at[r],
            device_id=(dpi(dest, x, zl), sq), device_id_type=MESH)

    def wy_wait(r):
        land = wbuf.at[lax.rem(y + NY - r, NY), x]
        pltpu.make_async_remote_copy(
            land, land, wy_s.at[r], wy_r.at[r],
            device_id=(dpi(y, x, zl), sq), device_id_type=MESH).wait_recv()

    def wx_copy(r):
        dest = lax.rem(x + r, NX)
        return pltpu.make_async_remote_copy(
            wbuf.at[:, x], wbuf.at[:, x], wx_s.at[r], wx_r.at[r],
            device_id=(dpi(y, dest, zl), sq), device_id_type=MESH)

    def wx_wait(r):
        land = wbuf.at[:, lax.rem(x + NX - r, NX)]
        pltpu.make_async_remote_copy(
            land, land, wx_s.at[r], wx_r.at[r],
            device_id=(dpi(y, x, zl), sq), device_id_type=MESH).wait_recv()

    for r in range(1, NY):
        wy_copy(r).start()

    og_copy.wait()
    gate_row = gate_ref[...].astype(jnp.float32)

    def gate_block(i, carry):
        rows = pl.ds(pl.multiple_of(i * 128, 128), 128)
        grad = (og[rows].astype(jnp.float32) * gate_row).astype(jnp.bfloat16)
        gpt[i] = grad.astype(jnp.float32).T.astype(jnp.bfloat16)
        return carry
    lax.fori_loop(0, TOK // 128, gate_block, 0)

    for r in range(1, NY):
        wy_wait(r)
    for r in range(1, NX):
        wx_copy(r).start()
    qkv_sent(0, 0)
    qkv_start(1, 1)
    qkv_start(1, 2)

    def attend(h):
        def body(it, carry):
            g = it // 2
            t = it % 2

            def qrow(i):
                return pl.ds(pl.multiple_of((t * GH + i) * (GW * TILE) + g * 96, 16), 96)

            def krow(i):
                return pl.ds(pl.multiple_of(i * (GW * TILE) + g * TILE, 16), 3 * TILE)

            queries = jnp.concatenate(
                [jnp.concatenate([qkv[h, 0, qrow(i)], bias[h, qrow(i)]], axis=1) for i in range(GH)], axis=0)
            keys = jnp.concatenate(
                [jnp.concatenate([qkv[h, 1, krow(i)], onehot[krow(i)]], axis=1) for i in range(GT * GH)], axis=0)
            values = jnp.concatenate([qkv[h, 2, krow(i)] for i in range(GT * GH)], axis=0)
            scores = lax.dot_general(
                queries, keys, (((1,), (1,)), ((), ())), preferred_element_type=jnp.float32)
            peak = jnp.max(scores, axis=1, keepdims=True)
            weights = jnp.exp2((scores - peak) * SCALE2)
            share = 1.0 / jnp.sum(weights, axis=1, keepdims=True)
            probs = (weights * share).astype(jnp.bfloat16)
            blended = jnp.dot(probs, values, preferred_element_type=jnp.float32).astype(jnp.bfloat16)
            for i in range(GH):
                att[2 * sq + h, qrow(i)] = blended[i * 96:(i + 1) * 96]
            return carry
        lax.fori_loop(0, 4, body, 0)

    def piece(z_from, core, h, half):
        return att.at[2 * sqi(z_from, core) + h, pl.ds(half * HALF, HALF)]

    def ag_direct(way, h, half):
        ref = piece(zh, c, h, half)
        step = 1 if way == 0 else -1
        return pltpu.make_async_remote_copy(
            ref, ref, agd_s.at[way, h, half], agd_r.at[way, h, half],
            device_id=(dp, sqi(zh + step, c)), device_id_type=MESH)

    def ag_direct_wait(way, h, half):
        ref = piece(zh - 1 if way == 0 else zh + 1, c, h, half)
        pltpu.make_async_remote_copy(
            ref, ref, agd_s.at[way, h, half], agd_r.at[way, h, half],
            device_id=(dp, sq), device_id_type=MESH).wait_recv()

    def ag_forward(h, half):
        ref = piece(zh - 1 if half == 0 else zh + 1, c, h, half)
        step = 1 if half == 0 else -1
        return pltpu.make_async_remote_copy(
            ref, ref, agf_s.at[h, half], agf_r.at[h, half],
            device_id=(dp, sqi(zh + step, c)), device_id_type=MESH)

    def ag_forward_wait(h, half):
        ref = piece(zh + 2, c, h, half)
        pltpu.make_async_remote_copy(
            ref, ref, agf_s.at[h, half], agf_r.at[h, half],
            device_id=(dp, sq), device_id_type=MESH).wait_recv()

    away = (0, -1, 1, 2)

    def ag_core(rel, h, half):
        ref = piece(zh + away[rel], c, h, half)
        return pltpu.make_async_remote_copy(
            ref, ref, agc_s.at[rel, h, half], agc_r.at[rel, h, half],
            device_id=(dp, zh * 2 + 1 - c), device_id_type=MESH)

    def ag_core_wait(rel, h):
        for half in range(2):
            ref = piece(zh + away[rel], 1 - c, h, half)
            pltpu.make_async_remote_copy(
                ref, ref, agc_s.at[rel, h, half], agc_r.at[rel, h, half],
                device_id=(dp, sq), device_id_type=MESH).wait_recv()

    def send_own(h):
        ag_direct(0, h, 0).start()
        ag_direct(1, h, 1).start()
        ag_direct(0, h, 1).start()
        ag_direct(1, h, 0).start()
        ag_core(0, h, 0).start()
        ag_core(0, h, 1).start()

    def relay_first(h):
        ag_direct_wait(0, h, 0)
        ag_forward(h, 0).start()
        ag_core(1, h, 0).start()
        ag_direct_wait(1, h, 1)
        ag_forward(h, 1).start()
        ag_core(2, h, 1).start()

    def relay_second(h):
        ag_direct_wait(0, h, 1)
        ag_core(1, h, 1).start()
        ag_direct_wait(1, h, 0)
        ag_core(2, h, 0).start()

    def relay_far(h):
        for half in range(2):
            ag_forward_wait(h, half)
            ag_core(3, h, half).start()

    chunk_of = [
        sqi(zh, c), sqi(zh, 1 - c), sqi(zh - 1, c), sqi(zh - 1, 1 - c),
        sqi(zh + 1, c), sqi(zh + 1, 1 - c), sqi(zh + 2, c), sqi(zh + 2, 1 - c),
    ]

    partner = x + 1 - 2 * lax.rem(x, 2)

    def xs_copy(n, h):
        return pltpu.make_async_remote_copy(
            xs.at[n, h], xr.at[n, h], xs_sem.at[n, h], xr_sem.at[n, h],
            device_id=(dpi(y, partner, zl), sq), device_id_type=MESH)

    def xf_copy(n):
        return pltpu.make_async_remote_copy(
            xf.at[n], xg.at[n], xf_sem.at[n], xg_sem.at[n],
            device_id=(dpi(y, NX - 1 - x, zl), sq), device_id_type=MESH)

    def head_rows(pair, rows):
        return jnp.concatenate([att[2 * chunk_of[n] + h, rows] for n, h in pair], axis=1)

    def grad_pair(pair):
        total = jnp.zeros((COLS, 256), jnp.float32)
        for i in range(TOK // 128):
            total += jnp.dot(gpt[i], head_rows(pair, pl.ds(i * 128, 128)), preferred_element_type=jnp.float32)
        turned[...] = total.T
        for i, (n, h) in enumerate(pair):
            kept = lax.rem(x // 2 + h + x, 2)
            own[n, h] = turned[pl.ds(pl.multiple_of(i * 128 + kept * 64, 64), 64)]
            xs[n, h] = turned[pl.ds(pl.multiple_of(i * 128 + (1 - kept) * 64, 64), 64)].astype(jnp.bfloat16)
            xs_copy(n, h).start()

    def project_pair(pair, first=False, last=False):
        weight = jnp.concatenate(
            [wbuf[chunk_of[n], 2 * h:2 * h + 2].reshape(128, COLS) for n, h in pair], axis=0)

        def body(i, carry):
            rows = pl.ds(pl.multiple_of(i * 288, 16), 288)
            value = jnp.dot(head_rows(pair, rows), weight, preferred_element_type=jnp.float32)
            if first:
                acc[rows] = value
            elif last:
                out_ref[rows] = ((acc[rows] + value) * gate_row).astype(jnp.bfloat16)
            else:
                acc[rows] += value
            return carry
        lax.fori_loop(0, TOK // 288, body, 0)

    def ys_copy(n, side):
        s = chunk_of[n]
        r = lax.rem(s + NY - y, NY)
        target = zl if side == 0 else 1 - zl
        return pltpu.make_async_remote_copy(
            ys.at[n, side], yr.at[side, r], ys_sem.at[n, side], yr_sem.at[side, r],
            device_id=(dpi(s, x, target), sq), device_id_type=MESH)

    def near_sum(n, h):
        xs_copy(n, h).wait_recv()
        return own[n, h] + xr[n, h].astype(jnp.float32)

    def middle_pair(pair):
        for n, h in pair:
            @pl.when(x // 2 != h)
            def _(n=n, h=h):
                xf[n] = near_sum(n, h).astype(jnp.bfloat16)
                xf_copy(n).start()

    def reduce_pair(pair):
        for n, h in pair:
            @pl.when(x // 2 == h)
            def _(n=n, h=h):
                near = near_sum(n, h)
                xf_copy(n).wait_recv()
                total[...] = near + xg[n].astype(jnp.float32)
                mine = total[pl.ds(pl.multiple_of(zl * WROWS, 8), WROWS)]
                ys[n, 1] = total[pl.ds(pl.multiple_of((1 - zl) * WROWS, 8), WROWS)].astype(jnp.bfloat16)
                ys_copy(n, 1).start()

                @pl.when(chunk_of[n] == y)
                def _():
                    yo[...] = mine

                @pl.when(chunk_of[n] != y)
                def _():
                    ys[n, 0] = mine.astype(jnp.bfloat16)
                    ys_copy(n, 0).start()

    def drain_pair(pair):
        for n, h in pair:
            xs_copy(n, h).wait_send()

            @pl.when(x // 2 != h)
            def _(n=n):
                xf_copy(n).wait_send()

    def drain_ag(h):
        for half in range(2):
            for way in range(2):
                ag_direct(way, h, half).wait_send()
            ag_forward(h, half).wait_send()
            for rel in range(4):
                ag_core(rel, h, half).wait_send()

    def qkv_arrive(h):
        for t in range(3):
            pltpu.make_async_copy(
                qkv.at[h, t, pl.ds(0, ROWS)], qkv.at[h, t, pl.ds(0, ROWS)], qr_sem.at[h, t, 0]).wait()

        def wait_one(r, carry):
            for t in range(3):
                qkv_wait(h, t, r)
            return carry
        lax.fori_loop(1, NS, wait_one, 0)

    pair_a, pair_b = ((0, 0), (0, 1)), ((1, 0), (1, 1))
    pair_c, pair_d, pair_e = ((2, 0), (3, 0)), ((4, 0), (5, 0)), ((6, 0), (7, 0))
    pair_f, pair_g, pair_h = ((2, 1), (3, 1)), ((4, 1), (5, 1)), ((6, 1), (7, 1))

    qkv_arrive(0)
    attend(0)
    send_own(0)
    qkv_arrive(1)
    relay_first(0)
    attend(1)
    send_own(1)
    for r in range(1, NX):
        wx_wait(r)
    grad_pair(pair_a)
    project_pair(pair_a, first=True)
    relay_second(0)
    for h in range(2):
        ag_core_wait(0, h)
    grad_pair(pair_b)
    project_pair(pair_b)
    middle_pair(pair_a)
    ag_core_wait(1, 0)
    grad_pair(pair_c)
    project_pair(pair_c)
    middle_pair(pair_b)
    ag_core_wait(2, 0)
    grad_pair(pair_d)
    project_pair(pair_d)
    relay_far(0)
    relay_first(1)
    middle_pair(pair_c)
    w_z.wait_send()
    for r in range(1, NY):
        wy_copy(r).wait_send()
    for r in range(1, NX):
        wx_copy(r).wait_send()
    qkv_sent(0, 1)
    qkv_sent(0, 2)
    qkv_sent(1, 0)
    qkv_sent(1, 1)
    qkv_sent(1, 2)
    ag_core_wait(3, 0)
    grad_pair(pair_e)
    project_pair(pair_e)
    middle_pair(pair_d)
    relay_second(1)
    middle_pair(pair_e)
    ag_core_wait(1, 1)
    grad_pair(pair_f)
    ag_core_wait(2, 1)
    grad_pair(pair_g)
    project_pair(pair_f)
    middle_pair(pair_f)
    project_pair(pair_g)
    middle_pair(pair_g)
    drain_ag(0)
    for pair in (pair_a, pair_b, pair_c, pair_d, pair_e):
        drain_pair(pair)
    relay_far(1)
    reduce_pair(pair_a)
    reduce_pair(pair_b)
    reduce_pair(pair_c)
    reduce_pair(pair_d)
    reduce_pair(pair_e)
    ag_core_wait(3, 1)
    grad_pair(pair_h)
    reduce_pair(pair_f)
    reduce_pair(pair_g)
    middle_pair(pair_h)
    project_pair(pair_h, last=True)
    drain_pair(pair_f)
    drain_pair(pair_g)
    drain_ag(1)
    reduce_pair(pair_h)

    summed = yo[...]
    for side in range(2):
        for r in range(1 - side, NY):
            pltpu.make_async_remote_copy(
                yr.at[side, r], yr.at[side, r], ys_sem.at[0, 0], yr_sem.at[side, r],
                device_id=(dp, sq), device_id_type=MESH).wait_recv()
            summed += yr[side, r].astype(jnp.float32)
    wg_ref[...] = summed

    drain_pair(pair_h)
    for n in range(NS):
        ys_copy(n, 1).wait_send()

        @pl.when(chunk_of[n] != y)
        def _(n=n):
            ys_copy(n, 0).wait_send()


def per_device(query_rows, key_rows, value_rows, windows, out_weight, gate_scale, out_grad):
    anywhere = pl.BlockSpec(memory_space=pl.ANY)
    vmem = pl.BlockSpec(memory_space=pltpu.VMEM)
    smem = pl.BlockSpec(memory_space=pltpu.SMEM)
    bf16, f32 = jnp.bfloat16, jnp.float32
    dma = pltpu.SemaphoreType.DMA
    return pl.pallas_call(
        kernel,
        out_shape=(
            pltpu.VMEM((TOK, COLS), bf16),
            pltpu.VMEM((WROWS, COLS), f32),
        ),
        in_specs=[anywhere, anywhere, anywhere, smem, anywhere, vmem, anywhere],
        out_specs=(vmem, vmem),
        scratch_shapes=[
            pltpu.VMEM((2, 3, TOK, HEAD_DIM), bf16),
            pltpu.VMEM((TOK, 128), bf16),
            pltpu.VMEM((2, TOK, 128), bf16),
            pltpu.VMEM((2 * NS, TOK, HEAD_DIM), bf16),
            pltpu.VMEM((NY, NX, NZ, WROWS, COLS), bf16),
            pltpu.VMEM((TOK, COLS), bf16),
            pltpu.VMEM((TOK // 128, COLS, 128), bf16),
            pltpu.VMEM((TOK, COLS), f32),
            pltpu.VMEM((256, COLS), f32),
            pltpu.VMEM((NS, 2, 64, COLS), f32),
            pltpu.VMEM((NS, 2, 64, COLS), bf16),
            pltpu.VMEM((NS, 2, 64, COLS), bf16),
            pltpu.VMEM((NS, 64, COLS), bf16),
            pltpu.VMEM((NS, 64, COLS), bf16),
            pltpu.VMEM((NS, 2, WROWS, COLS), bf16),
            pltpu.VMEM((2, NY, WROWS, COLS), bf16),
            pltpu.VMEM((WROWS, COLS), f32),
            pltpu.VMEM((64, COLS), f32),
            dma((2, 3, NS)), dma((2, 3, NS)), dma((2,)), dma((2,)),
            dma((NY,)), dma((NY,)), dma((NX,)), dma((NX,)),
            dma((2, 2, 2)), dma((2, 2, 2)), dma((2, 2)), dma((2, 2)),
            dma((4, 2, 2)), dma((4, 2, 2)),
            dma((NS, 2)), dma((NS, 2)), dma((NS,)), dma((NS,)), dma((NS, 2)), dma((2, NY)),
        ],
        compiler_params=pltpu.CompilerParams(
            collective_id=0, has_side_effects=True, vmem_limit_bytes=56 * 1024 * 1024),
        name="video_attention_block",
    )(query_rows, key_rows, value_rows, windows.T, out_weight, gate_scale, out_grad)


def solution(mesh):
    return jax.shard_map(
        per_device,
        mesh=mesh,
        in_specs=(
            P(("dp", "seq"), None),
            P(("dp", "seq"), None),
            P(("dp", "seq"), None),
            P(),
            P("dp", "seq"),
            P("dp", "seq"),
            P("dp", "seq"),
        ),
        out_specs=(P("dp", "seq"), P("dp", "seq")),
        check_vma=False,
    )
```
